32 devices in a mesh: seq: 4 (over y, core), nbr: 8 (over z, x).
Axes of the slice: x: 2, y: 2, z: 4, core: 2. Of those that a mesh axis runs over, the one named last changes fastest.
Arguments:
- queries: bfloat16 [8192, 2048], P(('seq', 'nbr')), may hold values from -16 to 16
- cotangent: bfloat16 [8192, 2048], P(('seq', 'nbr')), may hold values from -6 to 6
- neighbour_tokens: bfloat16 [256, 128, 896], P(('seq', 'nbr')), may hold values from -6 to 6
- neighbour_ids: int32 [128, 2], P(('seq', 'nbr')), may hold values from 0 to 255, as said below
- neighbour_dest: int32 [256], P(('seq', 'nbr')), may hold values from 0 to 255, as said below
- sequence_ids: int32 [128], P(('seq', 'nbr')), may hold values from 0 to 7, never falling along the last dimension, each value on 1 to 32 neighbouring positions
- enc_in: bfloat16 [896, 1792], replicated, may hold values from -0.1875 to 0.1875
- enc_out: bfloat16 [1792, 896], replicated, may hold values from -0.125 to 0.125
- key_weight: bfloat16 [896, 2048], replicated, may hold values from -0.5 to 0.5
- value_weight: bfloat16 [896, 2048], replicated, may hold values from -0.1875 to 0.1875
Outputs:
- attended: bfloat16 [8192, 2048], P(('seq', 'nbr'))
- grad_encoded: bfloat16 [256, 128, 896], P(('seq', 'nbr'))
The draws below stay inside these ranges and needn't reach their ends.
Inputs may be any that keep to these rules, and one draw needn't show every extreme that they name: `neighbour_ids`: every number 0 to 255 appears exactly once. Neighbour n is held by device n // 8 in the order seq+nbr, a device of the same seq index as the device holding the span. Among the neighbours of one device's spans at most 2 are held by any one device, and in every draw some device has exactly 2 held by one device. neighbour_dest[neighbour_ids[c, k]] = c * 2 + k for every span c and k.
All inputs are finite; a program needn't handle non-finite values.
Results may differ from the reference program's by a relative error of at most 0.015.
The reference program's roundings to bfloat16 on the way count: a program that leaves them out, or rounds other values in their place, can miss the bound.
Values may be sent and summed in bfloat16 or wider, within the bound.
A program may use at most 128 MiB of HBM per device.

```python
import math
import jax
import jax.numpy as jnp
import numpy as np
from jax import lax

ENC = 896
HEAD_DIM = 128
HEADS = 16
ENC_FF = 1792
SPAN = 64
NEIGH_LEN = 128
TOPK = 2
CH_DEV = 4
NB_DEV = 8
SPANS = 128
TOKENS = 8192
NEIGHBOURS = 256
N_SEQ = 4
N_NBR = 8
DEVICES = 32


def one_group(group_key, group_idx):
    peer_count = N_NBR
    half_slots = NB_DEV // 2
    slot_total = peer_count * NB_DEV
    subkeys = jax.random.split(group_key, 6)
    first_set = jax.random.permutation(subkeys[0], peer_count)[:half_slots]
    relabel = jax.random.permutation(subkeys[1], peer_count)
    source = jax.random.randint(subkeys[2], (), 0, peer_count)
    target = (source + first_set[0]) % peer_count
    wanted = (relabel[target] - relabel[source]) % peer_count
    shuffled = jax.random.permutation(subkeys[3], peer_count)
    position = jnp.argmax(shuffled == wanted)
    swapped = shuffled.at[position].set(shuffled[0]).at[0].set(wanted)
    second = swapped[:half_slots]
    inverse = jnp.argsort(relabel)
    row_index = jnp.arange(peer_count)
    owners_a = (row_index[:, None] + first_set[None, :]) % peer_count
    owners_b = inverse[(relabel[:, None] + second[None, :]) % peer_count]
    owners = jnp.concatenate([owners_a, owners_b], axis=1)
    row_keys = jax.random.split(subkeys[4], peer_count)
    shuffle = jax.vmap(lambda row_key: jax.random.permutation(row_key, NB_DEV))(row_keys)
    owners = jnp.take_along_axis(owners, shuffle, axis=1).reshape(-1)
    scores = owners * slot_total + jax.random.permutation(subkeys[5], slot_total)
    placing = jnp.argsort(jnp.argsort(scores))
    local_idx = placing - owners * NB_DEV
    return ((group_idx * peer_count + owners) * NB_DEV + local_idx).astype(jnp.int32)


def routing(key):
    group_keys = jax.random.split(jax.random.fold_in(key, 7), N_SEQ)
    grouped = jax.vmap(one_group)(group_keys, jnp.arange(N_SEQ))
    return grouped.reshape(-1).astype(jnp.int32)


def draw_neighbour_ids(key, part):
    return routing(key).reshape(SPANS, TOPK)


def draw_neighbour_dest(key, part):
    return jnp.argsort(routing(key)).astype(jnp.int32)


def draw_queries(key, part):
    base_key = jax.random.fold_in(jax.random.fold_in(key, 11), 0)
    base_draw = jax.random.truncated_normal(base_key, -6.0, 6.0, (TOKENS, HEADS * HEAD_DIM), jnp.float32)
    return base_draw.astype(jnp.bfloat16)


def level_of(rng, extent, cuts, least, top_value):
    def one(axis_at, parts):
        draws = jax.random.uniform(jax.random.fold_in(jax.random.fold_in(rng, 6), axis_at), (parts,), jnp.float32, least / len(cuts), top_value / len(cuts))
        return jnp.repeat(jnp.exp(draws), extent[axis_at] // parts).reshape((-1,) + (1,) * (len(extent) - axis_at - 1))

    level = one(*cuts[0])
    for cut in cuts[1:]:
        level = level * one(*cut)
    return level


def length_profile(amount, total, most, skew):
    portions = [(1 << 20) // math.isqrt(grade ** skew) + 1 for grade in range(2, amount + 1)]
    rest, counts = total - most - (amount - 1), [1] * (amount - 1)
    while rest > 0:
        free = [i for i in range(amount - 1) if counts[i] < most]
        pool, budget = sum([portions[i] for i in free]), rest
        for i in free:
            extra = min(most - counts[i], max(1, budget * portions[i] // pool), rest)
            counts[i] = counts[i] + extra
            rest = rest - extra
    return np.array([most] + counts)


def uneven(stream_key, count, total, most, slope):
    if count == 2:
        one = jax.random.randint(stream_key, (), max(1, total - most), min(most, total - 1) + 1)
        return jnp.stack([one, total - one])
    lengths = jnp.asarray(length_profile(count, total, most, slope), jnp.int32)
    twos = (count - 1) // 2
    giver, receiver = lengths[1:1 + 2 * twos:2], lengths[2:2 + 2 * twos:2]
    room = jnp.minimum(giver - 1, most - receiver)
    moved = jax.random.randint(jax.random.fold_in(stream_key, 1), (twos,), 0, 1 << 20) % (room + 1)
    lengths = lengths.at[1:1 + 2 * twos:2].set(giver - moved).at[2:2 + 2 * twos:2].set(receiver + moved)
    return lengths[jax.random.permutation(jax.random.fold_in(stream_key, 2), count)]


def scatter_about(stream_key, dims, width, limit, shards=(), held_as=jnp.bfloat16):
    values = jax.random.normal(stream_key, dims, jnp.float32) * width
    if len(shards) > 0:
        values = level_of(stream_key, dims, shards, -0.22, 0.18) * values
    return jnp.clip(values, min=-limit, max=limit).astype(held_as)


def setup_inputs(seed: int = 0) -> dict:
    keys = jax.random.split(jax.random.key(seed), 11)
    return {
        "queries": draw_queries(jax.random.fold_in(keys[10], 71), 0),
        "cotangent": scatter_about(keys[1], (TOKENS, HEADS * HEAD_DIM), 1.0, 6.0, ((0, 32),)),
        "neighbour_tokens": scatter_about(keys[2], (NEIGHBOURS, NEIGH_LEN, ENC), 1.0, 6.0, ((0, 32),)),
        "neighbour_ids": draw_neighbour_ids(jax.random.fold_in(keys[10], 71), 0),
        "neighbour_dest": draw_neighbour_dest(jax.random.fold_in(keys[10], 71), 0),
        "sequence_ids": jnp.searchsorted(jnp.cumsum(uneven(keys[5], SPANS // 16, SPANS, 32, 2)), jnp.arange(SPANS), side="right").astype(jnp.int32),
        "enc_in": scatter_about(keys[6], (ENC, ENC_FF), ENC ** -0.5, 0.1875),
        "enc_out": scatter_about(keys[7], (ENC_FF, ENC), ENC_FF ** -0.5, 0.125),
        "key_weight": scatter_about(keys[8], (ENC, HEADS * HEAD_DIM), (ENC // 8) ** -0.5, 0.5),
        "value_weight": scatter_about(keys[9], (ENC, HEADS * HEAD_DIM), ENC ** -0.5, 0.1875),
    }


epsilon = 1e-06

def as_float(values_in):
    return lax.optimization_barrier(values_in).astype(jnp.float32)

def encode(block, enc_in, enc_out):
    inputs = block.astype(jnp.float32)
    scaling = lax.rsqrt(lax.optimization_barrier(jnp.mean(inputs * inputs, axis=-1, keepdims=True)) + epsilon)
    normed = (inputs * scaling).astype(jnp.bfloat16)
    hidden_act = jax.nn.gelu(jnp.dot(normed, enc_in, preferred_element_type=jnp.float32), approximate=True).astype(jnp.bfloat16)
    return (inputs + jnp.dot(hidden_act, enc_out, preferred_element_type=jnp.float32)).astype(jnp.bfloat16)

def attend(query_rows, cot_rows, slot_block, validity, key_weight, value_weight):
    blocks, span_len, features = query_rows.shape
    head_count = features // HEAD_DIM
    slot_count, length, enc_width = slot_block.shape
    flat_slots = slot_block.reshape(slot_count * length, enc_width)
    key_rows = jnp.dot(flat_slots, key_weight, preferred_element_type=jnp.float32).astype(jnp.bfloat16)
    value_rows = jnp.dot(flat_slots, value_weight, preferred_element_type=jnp.float32).astype(jnp.bfloat16)
    key_rows = as_float(key_rows).reshape(blocks, -1, head_count, HEAD_DIM)
    value_rows = as_float(value_rows).reshape(blocks, -1, head_count, HEAD_DIM)
    query_four = query_rows.astype(jnp.float32).reshape(blocks, span_len, head_count, HEAD_DIM)
    inv_root = 1.0 / math.sqrt(HEAD_DIM)
    scores = jnp.einsum('cmhd,cphd->chmp', query_four, key_rows) * inv_root
    shares = jax.nn.softmax(scores, axis=-1)
    weights = as_float(shares.astype(jnp.bfloat16))
    mixture = jnp.einsum('chmp,cphd->cmhd', weights, value_rows)
    attended = (mixture * validity[:, :, None, None]).astype(jnp.bfloat16).reshape(blocks, span_len, features)
    masked = cot_rows.astype(jnp.float32).reshape(blocks, span_len, head_count, HEAD_DIM) * validity[:, :, None, None]
    grad_weights = jnp.einsum('cmhd,cphd->chmp', masked, value_rows)
    grad_scores = shares * (grad_weights - lax.optimization_barrier(jnp.sum(shares * grad_weights, axis=-1, keepdims=True)))
    grad_scores = as_float(grad_scores.astype(jnp.bfloat16))
    grad_keys = (jnp.einsum('chmp,cmhd->cphd', grad_scores, query_four) * inv_root).astype(jnp.bfloat16)
    grad_values = jnp.einsum('chmp,cmhd->cphd', weights, masked).astype(jnp.bfloat16)
    grad_keys = grad_keys.reshape(slot_count * length, features)
    grad_values = grad_values.reshape(slot_count * length, features)
    slot_grads = jnp.dot(grad_keys, key_weight.T, preferred_element_type=jnp.float32) + jnp.dot(grad_values, value_weight.T, preferred_element_type=jnp.float32)
    return (attended, slot_grads.astype(jnp.bfloat16).reshape(slot_count, length, enc_width))

def reference(queries, cotangent, neighbour_tokens, neighbour_ids, neighbour_dest, sequence_ids, enc_in, enc_out, key_weight, value_weight):
    length = neighbour_tokens.shape[1]
    enc_width = neighbour_tokens.shape[2]
    features = queries.shape[1]
    blocks_in = neighbour_tokens.reshape(DEVICES, NB_DEV * length, enc_width)
    encoded = lax.map(lambda block: encode(block, enc_in, enc_out), blocks_in).reshape(NEIGHBOURS, length, enc_width)
    head_rows = SPAN - 1
    pad_rows = jnp.zeros((head_rows, features), queries.dtype)
    query_ext = jnp.concatenate([queries[head_rows:], pad_rows], 0).reshape(DEVICES, CH_DEV, SPAN, features)
    cot_ext = jnp.concatenate([cotangent[head_rows:], pad_rows], 0).reshape(DEVICES, CH_DEV, SPAN, features)
    later_ids = jnp.concatenate([sequence_ids[1:], jnp.full((1,), -1, jnp.int32)], 0)
    offsets = jnp.arange(SPAN)
    validity = ((offsets[None, :] == 0) | (sequence_ids[:, None] == later_ids[:, None])).astype(jnp.float32)
    validity = validity.reshape(DEVICES, CH_DEV, SPAN)
    slot_ids = neighbour_ids.reshape(DEVICES, NB_DEV).astype(jnp.int32)

    def one_block(inputs):
        query_rows, cot_rows, valid_rows, indices = inputs
        slot_block = jnp.take(encoded, indices, axis=0)
        return attend(query_rows, cot_rows, slot_block, valid_rows, key_weight, value_weight)
    attended_ext, slot_grads = lax.map(one_block, (query_ext, cot_ext, validity, slot_ids))
    attended_ext = attended_ext.reshape(TOKENS, features)
    attended = jnp.concatenate([pad_rows, attended_ext[:TOKENS - head_rows]], 0)
    grad_encoded = jnp.take(slot_grads.reshape(SPANS * TOPK, length, enc_width), neighbour_dest.astype(jnp.int32), axis=0)
    return (attended, grad_encoded)
```

```python
import functools
import math

import jax
import jax.numpy as jnp
from jax import lax
from jax.experimental import pallas as pl
from jax.experimental.pallas import tpu as pltpu
from jax.sharding import PartitionSpec as P

HEAD_DIM = 128
CAP = 2
CHUNK = 256
PARTS = 2


epsilon = 1e-06

NT = (((1,), (1,)), ((), ()))
TN = (((0,), (0,)), ((), ()))


def from_behind(block, axis, distance):
    devices = range(lax.axis_size(axis))
    route = [(i - distance, i) for i in devices if i - distance in devices]
    return lax.ppermute(block, axis, route)


def dot(a, b, dims=(((1,), (0,)), ((), ()))):
    return lax.dot_general(a, b, dims, preferred_element_type=jnp.float32)


def encode_kernel(slot_ref, x_ref, in_ref, out_w_ref, out_ref, normed, acc):
    step = pl.program_id(0)
    count, rows, width = x_ref.shape

    @pl.when(step == 0)
    def _():
        inputs = x_ref[...].reshape(count * rows, width).astype(jnp.float32)
        scaling = lax.rsqrt(jnp.mean(inputs * inputs, axis=-1, keepdims=True) + epsilon)
        normed[...] = (inputs * scaling).astype(jnp.bfloat16)
        acc[...] = inputs

    hidden = jax.nn.gelu(dot(normed[...], in_ref[...]), approximate=True).astype(jnp.bfloat16)
    acc[...] += dot(hidden, out_w_ref[...])

    @pl.when(step == pl.num_programs(0) - 1)
    def _():
        for n in range(count):
            out_ref[slot_ref[n]] = acc[n * rows : (n + 1) * rows].astype(jnp.bfloat16)


def encode_part(part, tokens, enc_in, enc_out, send_slot, slot_total):
    count, length, width = tokens.shape
    rows = length // PARTS
    hidden = enc_in.shape[1]
    return pl.pallas_call(
        encode_kernel,
        grid_spec=pltpu.PrefetchScalarGridSpec(
            num_scalar_prefetch=1,
            grid=(hidden // CHUNK,),
            in_specs=[
                pl.BlockSpec((count, rows, width), lambda j, s: (0, part, 0)),
                pl.BlockSpec((width, CHUNK), lambda j, s: (0, j)),
                pl.BlockSpec((CHUNK, width), lambda j, s: (j, 0)),
            ],
            out_specs=pl.BlockSpec((slot_total, rows, width), lambda j, s: (0, 0, 0)),
            scratch_shapes=[
                pltpu.VMEM((count * rows, width), jnp.bfloat16),
                pltpu.VMEM((count * rows, width), jnp.float32),
            ],
        ),
        out_shape=jax.ShapeDtypeStruct((slot_total, rows, width), jnp.bfloat16),
        cost_estimate=pl.CostEstimate(
            flops=4 * count * rows * width * hidden,
            bytes_accessed=4 * width * hidden + 6 * count * rows * width,
            transcendentals=count * rows * hidden,
        ),
        name="encode_part",
    )(send_slot, tokens, enc_in, enc_out)


def gather_rows(slot_ref, x_ref, held, slots):
    rows = x_ref.shape[1]
    for n in range(slots):
        held[n * rows : (n + 1) * rows] = x_ref[slot_ref[n]]


def project_kernel(slots, slot_ref, x_ref, kw_ref, vw_ref, k_ref, v_ref, held):
    @pl.when(pl.program_id(0) == 0)
    def _():
        gather_rows(slot_ref, x_ref, held, slots)

    k_ref[...] = dot(held[...], kw_ref[...]).astype(jnp.bfloat16)
    v_ref[...] = dot(held[...], vw_ref[...]).astype(jnp.bfloat16)


def project_part(incoming, key_weight, value_weight, recv_slot):
    slot_total, rows, width = incoming.shape
    slots = recv_slot.shape[0]
    features = key_weight.shape[1]
    wide = 2 * CHUNK
    weight = pl.BlockSpec((width, wide), lambda j, s: (0, j))
    result = pl.BlockSpec((slots * rows, wide), lambda j, s: (0, j))
    shape = jax.ShapeDtypeStruct((slots * rows, features), jnp.bfloat16)
    return pl.pallas_call(
        functools.partial(project_kernel, slots),
        grid_spec=pltpu.PrefetchScalarGridSpec(
            num_scalar_prefetch=1,
            grid=(features // wide,),
            in_specs=[
                pl.BlockSpec((slot_total, rows, width), lambda j, s: (0, 0, 0)),
                weight,
                weight,
            ],
            out_specs=[result, result],
            scratch_shapes=[pltpu.VMEM((slots * rows, width), jnp.bfloat16)],
        ),
        out_shape=[shape, shape],
        cost_estimate=pl.CostEstimate(
            flops=4 * slots * rows * width * features,
            bytes_accessed=4 * width * features + 4 * slots * rows * features,
            transcendentals=0,
        ),
        name="project_part",
    )(recv_slot, incoming, key_weight, value_weight)


def attend_kernel(
    slots, spans, slot_ref, x_ref, ka_ref, va_ref, kw_ref, vw_ref, q_ref, c_ref, valid_ref,
    out_ref, gka_ref, gva_ref, gkb_ref, gvb_ref, held,
):
    @pl.when(pl.program_id(0) == 0)
    def _():
        gather_rows(slot_ref, x_ref, held, slots)

    inv_root = 1.0 / math.sqrt(HEAD_DIM)
    kb = dot(held[...], kw_ref[...]).astype(jnp.bfloat16)
    vb = dot(held[...], vw_ref[...]).astype(jnp.bfloat16)
    half = held.shape[0] // spans
    tokens = q_ref.shape[0] // spans
    for c in range(spans):
        near = slice(c * half, (c + 1) * half)
        mine = slice(c * tokens, (c + 1) * tokens)
        valid = valid_ref[mine]
        for h in range(q_ref.shape[1] // HEAD_DIM):
            cols = slice(h * HEAD_DIM, (h + 1) * HEAD_DIM)
            keys = jnp.concatenate([ka_ref[near, cols], kb[near, cols]], 0)
            values = jnp.concatenate([va_ref[near, cols], vb[near, cols]], 0)
            query = q_ref[mine, cols]
            masked = (c_ref[mine, cols].astype(jnp.float32) * valid).astype(jnp.bfloat16)
            scores = dot(query, keys, NT) * inv_root
            powers = jnp.exp(scores - jnp.max(scores, axis=-1, keepdims=True))
            shares = powers / jnp.sum(powers, axis=-1, keepdims=True)
            weights = shares.astype(jnp.bfloat16)
            out_ref[mine, cols] = (dot(weights, values) * valid).astype(jnp.bfloat16)
            grad_weights = dot(masked, values, NT)
            inner = jnp.sum(shares * grad_weights, axis=-1, keepdims=True)
            grad_scores = (shares * (grad_weights - inner)).astype(jnp.bfloat16)
            grad_keys = (dot(grad_scores, query, TN) * inv_root).astype(jnp.bfloat16)
            grad_values = dot(weights, masked, TN).astype(jnp.bfloat16)
            gka_ref[near, cols] = grad_keys[:half]
            gkb_ref[near, cols] = grad_keys[half:]
            gva_ref[near, cols] = grad_values[:half]
            gvb_ref[near, cols] = grad_values[half:]


def attend_all(incoming, keys_a, values_a, key_weight, value_weight, query, cot, valid, recv_slot):
    slot_total, rows, width = incoming.shape
    slots = recv_slot.shape[0]
    tokens, features = query.shape
    spans = valid.shape[0]
    column = valid.reshape(tokens, 1)
    weight = pl.BlockSpec((width, CHUNK), lambda j, s: (0, j))
    near = pl.BlockSpec((slots * rows, CHUNK), lambda j, s: (0, j))
    mine = pl.BlockSpec((tokens, CHUNK), lambda j, s: (0, j))
    shape = jax.ShapeDtypeStruct((slots * rows, features), jnp.bfloat16)
    positions = PARTS * slots * rows // spans
    return pl.pallas_call(
        functools.partial(attend_kernel, slots, spans),
        grid_spec=pltpu.PrefetchScalarGridSpec(
            num_scalar_prefetch=1,
            grid=(features // CHUNK,),
            in_specs=[
                pl.BlockSpec((slot_total, rows, width), lambda j, s: (0, 0, 0)),
                near,
                near,
                weight,
                weight,
                mine,
                mine,
                pl.BlockSpec((tokens, 1), lambda j, s: (0, 0)),
            ],
            out_specs=[mine, near, near, near, near],
            scratch_shapes=[pltpu.VMEM((slots * rows, width), jnp.bfloat16)],
        ),
        out_shape=[jax.ShapeDtypeStruct((tokens, features), jnp.bfloat16)] + [shape] * 4,
        cost_estimate=pl.CostEstimate(
            flops=4 * slots * rows * width * features + 10 * tokens * positions * features,
            bytes_accessed=4 * width * features + 12 * slots * rows * features,
            transcendentals=tokens * positions * features // HEAD_DIM,
        ),
        name="attend_all",
    )(recv_slot, incoming, keys_a, values_a, key_weight, value_weight, query, cot, column)


def return_kernel(slots, slot_ref, gk_ref, gv_ref, kw_ref, vw_ref, out_ref, acc):
    step = pl.program_id(0)

    @pl.when(step == 0)
    def _():
        acc[...] = jnp.zeros_like(acc)

    acc[...] += dot(gk_ref[...], kw_ref[...], NT) + dot(gv_ref[...], vw_ref[...], NT)

    @pl.when(step == pl.num_programs(0) - 1)
    def _():
        rows = out_ref.shape[1]
        for n in range(slots):
            out_ref[slot_ref[n]] = acc[n * rows : (n + 1) * rows].astype(jnp.bfloat16)


def return_part(grad_keys, grad_values, key_weight, value_weight, recv_slot, slot_total):
    slots = recv_slot.shape[0]
    total_rows, features = grad_keys.shape
    rows = total_rows // slots
    width = key_weight.shape[0]
    wide = 2 * CHUNK
    weight = pl.BlockSpec((width, wide), lambda j, s: (0, j))
    near = pl.BlockSpec((total_rows, wide), lambda j, s: (0, j))
    return pl.pallas_call(
        functools.partial(return_kernel, slots),
        grid_spec=pltpu.PrefetchScalarGridSpec(
            num_scalar_prefetch=1,
            grid=(features // wide,),
            in_specs=[near, near, weight, weight],
            out_specs=pl.BlockSpec((slot_total, rows, width), lambda j, s: (0, 0, 0)),
            scratch_shapes=[pltpu.VMEM((total_rows, width), jnp.float32)],
        ),
        out_shape=jax.ShapeDtypeStruct((slot_total, rows, width), jnp.bfloat16),
        cost_estimate=pl.CostEstimate(
            flops=4 * total_rows * width * features,
            bytes_accessed=4 * width * features + 4 * total_rows * features,
            transcendentals=0,
        ),
        name="return_part",
    )(recv_slot, grad_keys, grad_values, key_weight, value_weight)


def place_kernel(slot_ref, first_ref, second_ref, out_ref):
    rows = first_ref.shape[1]
    out_ref[0, :rows] = first_ref[0]
    out_ref[0, rows:] = second_ref[0]


def place(first, second, send_slot):
    _, rows, width = first.shape
    count = send_slot.shape[0]
    chosen = pl.BlockSpec((1, rows, width), lambda n, s: (s[n], 0, 0))
    return pl.pallas_call(
        place_kernel,
        grid_spec=pltpu.PrefetchScalarGridSpec(
            num_scalar_prefetch=1,
            grid=(count,),
            in_specs=[chosen, chosen],
            out_specs=pl.BlockSpec((1, PARTS * rows, width), lambda n, s: (n, 0, 0)),
        ),
        out_shape=jax.ShapeDtypeStruct((count, PARTS * rows, width), jnp.bfloat16),
        name="place",
    )(send_slot, first, second)


def exchange(block):
    return lax.all_to_all(block, "nbr", split_axis=0, concat_axis=0, tiled=True)


def shards(
    queries,
    cotangent,
    neighbour_tokens,
    neighbour_ids,
    neighbour_dest,
    sequence_ids,
    enc_in,
    enc_out,
    key_weight,
    value_weight,
):
    span_count = sequence_ids.shape[0]
    token_rows, features = queries.shape
    span_len = token_rows // span_count
    head_rows = span_len - 1
    nb_local = neighbour_tokens.shape[0]
    peer_count = lax.axis_size("nbr")
    slot_total = peer_count * CAP

    dest_peer = neighbour_dest // nb_local % peer_count
    earlier = jnp.arange(nb_local)
    same_dest = (dest_peer[:, None] == dest_peer[None, :]) & (earlier[None, :] < earlier[:, None])
    send_slot = dest_peer * CAP + jnp.sum(same_dest.astype(jnp.int32), axis=1)
    slot_ids = neighbour_ids.reshape(-1) % (peer_count * nb_local)
    owners = slot_ids // nb_local
    same_owner = (owners[:, None] == owners[None, :]) & (slot_ids[None, :] < slot_ids[:, None])
    recv_slot = owners * CAP + jnp.sum(same_owner.astype(jnp.int32), axis=1)

    sent_a = encode_part(0, neighbour_tokens, enc_in, enc_out, send_slot, slot_total)
    in_a = exchange(sent_a)
    sent_b = encode_part(1, neighbour_tokens, enc_in, enc_out, send_slot, slot_total)
    in_b = exchange(sent_b)

    label_send = (sequence_ids[:1] % 128 + 1).astype(jnp.bfloat16)
    next_query, next_cot, next_label = from_behind(
        (queries[:head_rows], cotangent[:head_rows], label_send), ("seq", "nbr"), -1
    )
    own_label = (sequence_ids % 128 + 1).astype(jnp.bfloat16)
    later_label = jnp.concatenate([own_label[1:], next_label], 0)
    offsets = jnp.arange(span_len)
    validity = ((offsets[None, :] == 0) | (own_label[:, None] == later_label[:, None])).astype(
        jnp.float32
    )
    query_ext = jnp.concatenate([queries[head_rows:], next_query], 0)
    cot_ext = jnp.concatenate([cotangent[head_rows:], next_cot], 0)

    keys_a, values_a = project_part(in_a, key_weight, value_weight, recv_slot)
    extended, gka, gva, gkb, gvb = attend_all(
        in_b, keys_a, values_a, key_weight, value_weight, query_ext, cot_ext, validity, recv_slot
    )
    back_a = exchange(return_part(gka, gva, key_weight, value_weight, recv_slot, slot_total))
    back_b = exchange(return_part(gkb, gvb, key_weight, value_weight, recv_slot, slot_total))
    carried = from_behind(extended[token_rows - head_rows :], ("seq", "nbr"), 1)
    attended = jnp.concatenate([carried, extended[: token_rows - head_rows]], 0)
    return (attended, place(back_a, back_b, send_slot))


def solution(mesh):
    in_specs = (
        P(("seq", "nbr"), None),
        P(("seq", "nbr"), None),
        P(("seq", "nbr"), None, None),
        P(("seq", "nbr"), None),
        P(("seq", "nbr")),
        P(("seq", "nbr")),
        P(),
        P(),
        P(),
        P(),
    )
    out_specs = (P(("seq", "nbr"), None), P(("seq", "nbr"), None, None))
    return jax.shard_map(shards, mesh=mesh, in_specs=in_specs, out_specs=out_specs, check_vma=False)
```

```python
import functools
import math

import jax
import jax.numpy as jnp
from jax import lax
from jax.experimental import pallas as pl
from jax.experimental.pallas import tpu as pltpu
from jax.sharding import PartitionSpec as P

HEAD_DIM = 128
CAP = 2
CHUNK = 256
PARTS = 2


epsilon = 1e-06

NT = (((1,), (1,)), ((), ()))
TN = (((0,), (0,)), ((), ()))


def from_behind(block, axis, distance):
    devices = range(lax.axis_size(axis))
    route = [(i - distance, i) for i in devices if i - distance in devices]
    return lax.ppermute(block, axis, route)


def dot(a, b, dims=(((1,), (0,)), ((), ()))):
    return lax.dot_general(a, b, dims, preferred_element_type=jnp.float32)


def encode_kernel(slot_ref, x_ref, in_ref, out_w_ref, out_ref, normed, acc):
    step = pl.program_id(0)
    count, rows, width = x_ref.shape

    @pl.when(step == 0)
    def _():
        inputs = x_ref[...].reshape(count * rows, width).astype(jnp.float32)
        scaling = lax.rsqrt(jnp.mean(inputs * inputs, axis=-1, keepdims=True) + epsilon)
        normed[...] = (inputs * scaling).astype(jnp.bfloat16)
        acc[...] = inputs

    hidden = jax.nn.gelu(dot(normed[...], in_ref[...]), approximate=True).astype(jnp.bfloat16)
    acc[...] += dot(hidden, out_w_ref[...])

    @pl.when(step == pl.num_programs(0) - 1)
    def _():
        for n in range(count):
            out_ref[slot_ref[n]] = acc[n * rows : (n + 1) * rows].astype(jnp.bfloat16)


def encode_part(part, tokens, enc_in, enc_out, send_slot, slot_total):
    count, length, width = tokens.shape
    rows = length // PARTS
    hidden = enc_in.shape[1]
    wide = hidden // 2
    return pl.pallas_call(
        encode_kernel,
        grid_spec=pltpu.PrefetchScalarGridSpec(
            num_scalar_prefetch=1,
            grid=(hidden // wide,),
            in_specs=[
                pl.BlockSpec((count, rows, width), lambda j, s: (0, part, 0)),
                pl.BlockSpec((width, wide), lambda j, s: (0, j)),
                pl.BlockSpec((wide, width), lambda j, s: (j, 0)),
            ],
            out_specs=pl.BlockSpec((slot_total, rows, width), lambda j, s: (0, 0, 0)),
            scratch_shapes=[
                pltpu.VMEM((count * rows, width), jnp.bfloat16),
                pltpu.VMEM((count * rows, width), jnp.float32),
            ],
        ),
        out_shape=jax.ShapeDtypeStruct((slot_total, rows, width), jnp.bfloat16),
        cost_estimate=pl.CostEstimate(
            flops=4 * count * rows * width * hidden,
            bytes_accessed=4 * width * hidden + 6 * count * rows * width,
            transcendentals=count * rows * hidden,
        ),
        name="encode_part",
    )(send_slot, tokens, enc_in, enc_out)


def gather_rows(slot_ref, x_ref, held, slots):
    rows = x_ref.shape[1]
    for n in range(slots):
        held[n * rows : (n + 1) * rows] = x_ref[slot_ref[n]]


def project_kernel(slots, slot_ref, x_ref, kw_ref, vw_ref, k_ref, v_ref, held):
    @pl.when(pl.program_id(0) == 0)
    def _():
        gather_rows(slot_ref, x_ref, held, slots)

    k_ref[...] = dot(held[...], kw_ref[...]).astype(jnp.bfloat16)
    v_ref[...] = dot(held[...], vw_ref[...]).astype(jnp.bfloat16)


def project_part(incoming, key_weight, value_weight, recv_slot):
    slot_total, rows, width = incoming.shape
    slots = recv_slot.shape[0]
    features = key_weight.shape[1]
    wide = 2 * CHUNK
    weight = pl.BlockSpec((width, wide), lambda j, s: (0, j))
    result = pl.BlockSpec((slots * rows, wide), lambda j, s: (0, j))
    shape = jax.ShapeDtypeStruct((slots * rows, features), jnp.bfloat16)
    return pl.pallas_call(
        functools.partial(project_kernel, slots),
        grid_spec=pltpu.PrefetchScalarGridSpec(
            num_scalar_prefetch=1,
            grid=(features // wide,),
            in_specs=[
                pl.BlockSpec((slot_total, rows, width), lambda j, s: (0, 0, 0)),
                weight,
                weight,
            ],
            out_specs=[result, result],
            scratch_shapes=[pltpu.VMEM((slots * rows, width), jnp.bfloat16)],
        ),
        out_shape=[shape, shape],
        cost_estimate=pl.CostEstimate(
            flops=4 * slots * rows * width * features,
            bytes_accessed=4 * width * features + 4 * slots * rows * features,
            transcendentals=0,
        ),
        name="project_part",
    )(recv_slot, incoming, key_weight, value_weight)


def attend_kernel(
    slots, spans, slot_ref, x_ref, ka_ref, va_ref, kw_ref, vw_ref, q_ref, c_ref, valid_ref,
    out_ref, gka_ref, gva_ref, gkb_ref, gvb_ref, held,
):
    @pl.when(pl.program_id(0) == 0)
    def _():
        gather_rows(slot_ref, x_ref, held, slots)

    inv_root = 1.0 / math.sqrt(HEAD_DIM)
    kb = dot(held[...], kw_ref[...]).astype(jnp.bfloat16)
    vb = dot(held[...], vw_ref[...]).astype(jnp.bfloat16)
    half = held.shape[0] // spans
    tokens = q_ref.shape[0] // spans
    units = [
        (
            slice(c * half, (c + 1) * half),
            slice(c * tokens, (c + 1) * tokens),
            slice(h * HEAD_DIM, (h + 1) * HEAD_DIM),
        )
        for c in range(spans)
        for h in range(q_ref.shape[1] // HEAD_DIM)
    ]
    keys = [jnp.concatenate([ka_ref[n, f], kb[n, f]], 0) for n, _, f in units]
    values = [jnp.concatenate([va_ref[n, f], vb[n, f]], 0) for n, _, f in units]
    masked = [
        (c_ref[m, f].astype(jnp.float32) * valid_ref[m]).astype(jnp.bfloat16) for _, m, f in units
    ]
    scores = [dot(q_ref[m, f], k, NT) * inv_root for (_, m, f), k in zip(units, keys)]
    grad_weights = [dot(g, v, NT) for g, v in zip(masked, values)]
    powers = [jnp.exp(x - jnp.max(x, axis=-1, keepdims=True)) for x in scores]
    shares = [x * (1.0 / jnp.sum(x, axis=-1, keepdims=True)) for x in powers]
    weights = [x.astype(jnp.bfloat16) for x in shares]
    grad_scores = [
        (x * (g - jnp.sum(x * g, axis=-1, keepdims=True))).astype(jnp.bfloat16)
        for x, g in zip(shares, grad_weights)
    ]
    for (_, m, f), w, v in zip(units, weights, values):
        out_ref[m, f] = (dot(w, v) * valid_ref[m]).astype(jnp.bfloat16)
    for (n, _, f), w, g in zip(units, weights, masked):
        grad_values = dot(w, g, TN).astype(jnp.bfloat16)
        gva_ref[n, f] = grad_values[:half]
        gvb_ref[n, f] = grad_values[half:]
    for (n, m, f), g in zip(units, grad_scores):
        grad_keys = (dot(g, q_ref[m, f], TN) * inv_root).astype(jnp.bfloat16)
        gka_ref[n, f] = grad_keys[:half]
        gkb_ref[n, f] = grad_keys[half:]


def attend_all(incoming, keys_a, values_a, key_weight, value_weight, query, cot, valid, recv_slot):
    slot_total, rows, width = incoming.shape
    slots = recv_slot.shape[0]
    tokens, features = query.shape
    spans = valid.shape[0]
    column = valid.reshape(tokens, 1)
    weight = pl.BlockSpec((width, CHUNK), lambda j, s: (0, j))
    near = pl.BlockSpec((slots * rows, CHUNK), lambda j, s: (0, j))
    mine = pl.BlockSpec((tokens, CHUNK), lambda j, s: (0, j))
    shape = jax.ShapeDtypeStruct((slots * rows, features), jnp.bfloat16)
    positions = PARTS * slots * rows // spans
    return pl.pallas_call(
        functools.partial(attend_kernel, slots, spans),
        grid_spec=pltpu.PrefetchScalarGridSpec(
            num_scalar_prefetch=1,
            grid=(features // CHUNK,),
            in_specs=[
                pl.BlockSpec((slot_total, rows, width), lambda j, s: (0, 0, 0)),
                near,
                near,
                weight,
                weight,
                mine,
                mine,
                pl.BlockSpec((tokens, 1), lambda j, s: (0, 0)),
            ],
            out_specs=[mine, near, near, near, near],
            scratch_shapes=[pltpu.VMEM((slots * rows, width), jnp.bfloat16)],
        ),
        out_shape=[jax.ShapeDtypeStruct((tokens, features), jnp.bfloat16)] + [shape] * 4,
        cost_estimate=pl.CostEstimate(
            flops=4 * slots * rows * width * features + 10 * tokens * positions * features,
            bytes_accessed=4 * width * features + 12 * slots * rows * features,
            transcendentals=tokens * positions * features // HEAD_DIM,
        ),
        name="attend_all",
    )(recv_slot, incoming, keys_a, values_a, key_weight, value_weight, query, cot, column)


def return_kernel(slots, slot_ref, gk_ref, gv_ref, kw_ref, vw_ref, out_ref, acc):
    step = pl.program_id(0)

    @pl.when(step == 0)
    def _():
        acc[...] = jnp.zeros_like(acc)

    acc[...] += dot(gk_ref[...], kw_ref[...], NT) + dot(gv_ref[...], vw_ref[...], NT)

    @pl.when(step == pl.num_programs(0) - 1)
    def _():
        rows = out_ref.shape[1]
        for n in range(slots):
            out_ref[slot_ref[n]] = acc[n * rows : (n + 1) * rows].astype(jnp.bfloat16)


def return_part(grad_keys, grad_values, key_weight, value_weight, recv_slot, slot_total):
    slots = recv_slot.shape[0]
    total_rows, features = grad_keys.shape
    rows = total_rows // slots
    width = key_weight.shape[0]
    wide = features // 2
    weight = pl.BlockSpec((width, wide), lambda j, s: (0, j))
    near = pl.BlockSpec((total_rows, wide), lambda j, s: (0, j))
    return pl.pallas_call(
        functools.partial(return_kernel, slots),
        grid_spec=pltpu.PrefetchScalarGridSpec(
            num_scalar_prefetch=1,
            grid=(features // wide,),
            in_specs=[near, near, weight, weight],
            out_specs=pl.BlockSpec((slot_total, rows, width), lambda j, s: (0, 0, 0)),
            scratch_shapes=[pltpu.VMEM((total_rows, width), jnp.float32)],
        ),
        out_shape=jax.ShapeDtypeStruct((slot_total, rows, width), jnp.bfloat16),
        cost_estimate=pl.CostEstimate(
            flops=4 * total_rows * width * features,
            bytes_accessed=4 * width * features + 4 * total_rows * features,
            transcendentals=0,
        ),
        name="return_part",
    )(recv_slot, grad_keys, grad_values, key_weight, value_weight)


def place_kernel(slot_ref, x_ref, *refs):
    out_ref = refs[-1]
    for n in range(out_ref.shape[0]):
        out_ref[n] = x_ref[slot_ref[n]]


def place(part, returned, send_slot, partial):
    slot_total, rows, width = returned.shape
    count = send_slot.shape[0]
    whole = [] if partial is None else [partial]
    return pl.pallas_call(
        place_kernel,
        grid_spec=pltpu.PrefetchScalarGridSpec(
            num_scalar_prefetch=1,
            grid=(1,),
            in_specs=[pl.BlockSpec((slot_total, rows, width), lambda n, s: (0, 0, 0))]
            + [pl.BlockSpec(memory_space=pl.ANY)] * len(whole),
            out_specs=pl.BlockSpec((count, rows, width), lambda n, s: (0, part, 0)),
        ),
        out_shape=jax.ShapeDtypeStruct((count, PARTS * rows, width), jnp.bfloat16),
        input_output_aliases={2: 0} if whole else {},
        name="place",
    )(send_slot, returned, *whole)


def exchange(block):
    return lax.all_to_all(block, "nbr", split_axis=0, concat_axis=0, tiled=True)


def shards(
    queries,
    cotangent,
    neighbour_tokens,
    neighbour_ids,
    neighbour_dest,
    sequence_ids,
    enc_in,
    enc_out,
    key_weight,
    value_weight,
):
    span_count = sequence_ids.shape[0]
    token_rows, features = queries.shape
    span_len = token_rows // span_count
    head_rows = span_len - 1
    nb_local = neighbour_tokens.shape[0]
    peer_count = lax.axis_size("nbr")
    slot_total = peer_count * CAP

    dest_peer = neighbour_dest // nb_local % peer_count
    earlier = jnp.arange(nb_local)
    same_dest = (dest_peer[:, None] == dest_peer[None, :]) & (earlier[None, :] < earlier[:, None])
    send_slot = dest_peer * CAP + jnp.sum(same_dest.astype(jnp.int32), axis=1)
    slot_ids = neighbour_ids.reshape(-1) % (peer_count * nb_local)
    owners = slot_ids // nb_local
    same_owner = (owners[:, None] == owners[None, :]) & (slot_ids[None, :] < slot_ids[:, None])
    recv_slot = owners * CAP + jnp.sum(same_owner.astype(jnp.int32), axis=1)

    label_send = (sequence_ids[:1] % 128 + 1).astype(jnp.bfloat16)
    next_query, next_cot, next_label = from_behind(
        (queries[:head_rows], cotangent[:head_rows], label_send), ("seq", "nbr"), -1
    )
    sent_a = encode_part(0, neighbour_tokens, enc_in, enc_out, send_slot, slot_total)
    sent_a, next_query, next_cot, next_label = lax.optimization_barrier(
        (sent_a, next_query, next_cot, next_label)
    )
    in_a = exchange(sent_a)
    sent_b = encode_part(1, neighbour_tokens, enc_in, enc_out, send_slot, slot_total)
    in_b = exchange(sent_b)
    own_label = (sequence_ids % 128 + 1).astype(jnp.bfloat16)
    later_label = jnp.concatenate([own_label[1:], next_label], 0)
    offsets = jnp.arange(span_len)
    validity = ((offsets[None, :] == 0) | (own_label[:, None] == later_label[:, None])).astype(
        jnp.float32
    )
    query_ext = jnp.concatenate([queries[head_rows:], next_query], 0)
    cot_ext = jnp.concatenate([cotangent[head_rows:], next_cot], 0)

    keys_a, values_a = project_part(in_a, key_weight, value_weight, recv_slot)
    extended, gka, gva, gkb, gvb = attend_all(
        in_b, keys_a, values_a, key_weight, value_weight, query_ext, cot_ext, validity, recv_slot
    )
    carried = from_behind(extended[token_rows - head_rows :], ("seq", "nbr"), 1)
    grads_a = return_part(gka, gva, key_weight, value_weight, recv_slot, slot_total)
    grads_a, carried = lax.optimization_barrier((grads_a, carried))
    back_a = exchange(grads_a)
    grads_b = return_part(gkb, gvb, key_weight, value_weight, recv_slot, slot_total)
    back_a, grads_b = lax.optimization_barrier((back_a, grads_b))
    back_b = exchange(grads_b)
    attended = jnp.concatenate([carried, extended[: token_rows - head_rows]], 0)
    grad_encoded = place(1, back_b, send_slot, place(0, back_a, send_slot, None))
    return (attended, grad_encoded)


def solution(mesh):
    in_specs = (
        P(("seq", "nbr"), None),
        P(("seq", "nbr"), None),
        P(("seq", "nbr"), None, None),
        P(("seq", "nbr"), None),
        P(("seq", "nbr")),
        P(("seq", "nbr")),
        P(),
        P(),
        P(),
        P(),
    )
    out_specs = (P(("seq", "nbr"), None), P(("seq", "nbr"), None, None))
    return jax.shard_map(shards, mesh=mesh, in_specs=in_specs, out_specs=out_specs, check_vma=False)
```

```python
import functools
import math

import jax
import jax.numpy as jnp
from jax import lax
from jax.experimental import pallas as pl
from jax.experimental.pallas import tpu as pltpu
from jax.sharding import PartitionSpec as P

HEAD_DIM = 128
CAP = 2
CHUNK = 256
PARTS = 2


epsilon = 1e-06

NT = (((1,), (1,)), ((), ()))
TN = (((0,), (0,)), ((), ()))


def from_behind(block, axis, distance):
    devices = range(lax.axis_size(axis))
    route = [(i - distance, i) for i in devices if i - distance in devices]
    return lax.ppermute(block, axis, route)


def dot(a, b, dims=(((1,), (0,)), ((), ()))):
    return lax.dot_general(a, b, dims, preferred_element_type=jnp.float32)


def encode_kernel(slot_ref, x_ref, in_ref, out_w_ref, out_ref, normed, acc):
    step = pl.program_id(0)
    count, rows, width = x_ref.shape

    @pl.when(step == 0)
    def _():
        inputs = x_ref[...].reshape(count * rows, width).astype(jnp.float32)
        scaling = lax.rsqrt(jnp.mean(inputs * inputs, axis=-1, keepdims=True) + epsilon)
        normed[...] = (inputs * scaling).astype(jnp.bfloat16)
        acc[...] = inputs

    hidden = jax.nn.gelu(dot(normed[...], in_ref[...]), approximate=True).astype(jnp.bfloat16)
    acc[...] += dot(hidden, out_w_ref[...])

    @pl.when(step == pl.num_programs(0) - 1)
    def _():
        for n in range(count):
            out_ref[slot_ref[n]] = acc[n * rows : (n + 1) * rows].astype(jnp.bfloat16)


def encode_part(part, tokens, enc_in, enc_out, send_slot, slot_total):
    count, length, width = tokens.shape
    rows = length // PARTS
    hidden = enc_in.shape[1]
    wide = hidden // 2
    return pl.pallas_call(
        encode_kernel,
        grid_spec=pltpu.PrefetchScalarGridSpec(
            num_scalar_prefetch=1,
            grid=(hidden // wide,),
            in_specs=[
                pl.BlockSpec((count, rows, width), lambda j, s: (0, part, 0)),
                pl.BlockSpec((width, wide), lambda j, s: (0, j)),
                pl.BlockSpec((wide, width), lambda j, s: (j, 0)),
            ],
            out_specs=pl.BlockSpec((slot_total, rows, width), lambda j, s: (0, 0, 0)),
            scratch_shapes=[
                pltpu.VMEM((count * rows, width), jnp.bfloat16),
                pltpu.VMEM((count * rows, width), jnp.float32),
            ],
        ),
        out_shape=jax.ShapeDtypeStruct((slot_total, rows, width), jnp.bfloat16),
        cost_estimate=pl.CostEstimate(
            flops=4 * count * rows * width * hidden,
            bytes_accessed=4 * width * hidden + 6 * count * rows * width,
            transcendentals=count * rows * hidden,
        ),
        name="encode_part",
    )(send_slot, tokens, enc_in, enc_out)


def gather_rows(slot_ref, x_ref, held, slots):
    rows = x_ref.shape[1]
    for n in range(slots):
        held[n * rows : (n + 1) * rows] = x_ref[slot_ref[n]]


def project_kernel(slots, slot_ref, x_ref, kw_ref, vw_ref, k_ref, v_ref, kt_ref, vt_ref, held):
    @pl.when(pl.program_id(0) == 0)
    def _():
        gather_rows(slot_ref, x_ref, held, slots)

    k_ref[...] = dot(held[...], kw_ref[...]).astype(jnp.bfloat16)
    v_ref[...] = dot(held[...], vw_ref[...]).astype(jnp.bfloat16)
    kt_ref[...] = kw_ref[...].T
    vt_ref[...] = vw_ref[...].T


def project_part(incoming, key_weight, value_weight, recv_slot):
    slot_total, rows, width = incoming.shape
    slots = recv_slot.shape[0]
    features = key_weight.shape[1]
    wide = 2 * CHUNK
    weight = pl.BlockSpec((width, wide), lambda j, s: (0, j))
    result = pl.BlockSpec((slots * rows, wide), lambda j, s: (0, j))
    shape = jax.ShapeDtypeStruct((slots * rows, features), jnp.bfloat16)
    turned = pl.BlockSpec((wide, width), lambda j, s: (j, 0))
    turned_shape = jax.ShapeDtypeStruct((features, width), jnp.bfloat16)
    return pl.pallas_call(
        functools.partial(project_kernel, slots),
        grid_spec=pltpu.PrefetchScalarGridSpec(
            num_scalar_prefetch=1,
            grid=(features // wide,),
            in_specs=[
                pl.BlockSpec((slot_total, rows, width), lambda j, s: (0, 0, 0)),
                weight,
                weight,
            ],
            out_specs=[result, result, turned, turned],
            scratch_shapes=[pltpu.VMEM((slots * rows, width), jnp.bfloat16)],
        ),
        out_shape=[shape, shape, turned_shape, turned_shape],
        cost_estimate=pl.CostEstimate(
            flops=4 * slots * rows * width * features,
            bytes_accessed=4 * width * features + 4 * slots * rows * features,
            transcendentals=0,
        ),
        name="project_part",
    )(recv_slot, incoming, key_weight, value_weight)


def attend_kernel(
    slots, spans, slot_ref, x_ref, ka_ref, va_ref, kw_ref, vw_ref, q_ref, c_ref, valid_ref,
    out_ref, gka_ref, gva_ref, gkb_ref, gvb_ref, held,
):
    @pl.when(pl.program_id(0) == 0)
    def _():
        gather_rows(slot_ref, x_ref, held, slots)

    inv_root = 1.0 / math.sqrt(HEAD_DIM)
    kb = dot(held[...], kw_ref[...]).astype(jnp.bfloat16)
    vb = dot(held[...], vw_ref[...]).astype(jnp.bfloat16)
    half = held.shape[0] // spans
    tokens = q_ref.shape[0] // spans
    units = [
        (
            slice(c * half, (c + 1) * half),
            slice(c * tokens, (c + 1) * tokens),
            slice(h * HEAD_DIM, (h + 1) * HEAD_DIM),
        )
        for c in range(spans)
        for h in range(q_ref.shape[1] // HEAD_DIM)
    ]
    keys = [jnp.concatenate([ka_ref[n, f], kb[n, f]], 0) for n, _, f in units]
    values = [jnp.concatenate([va_ref[n, f], vb[n, f]], 0) for n, _, f in units]
    masked = [
        (c_ref[m, f].astype(jnp.float32) * valid_ref[m]).astype(jnp.bfloat16) for _, m, f in units
    ]
    scores = [dot(q_ref[m, f], k, NT) * inv_root for (_, m, f), k in zip(units, keys)]
    grad_weights = [dot(g, v, NT) for g, v in zip(masked, values)]
    powers = [jnp.exp(x - jnp.max(x, axis=-1, keepdims=True)) for x in scores]
    shares = [x * (1.0 / jnp.sum(x, axis=-1, keepdims=True)) for x in powers]
    weights = [x.astype(jnp.bfloat16) for x in shares]
    grad_scores = [
        (x * (g - jnp.sum(x * g, axis=-1, keepdims=True))).astype(jnp.bfloat16)
        for x, g in zip(shares, grad_weights)
    ]
    for (_, m, f), w, v in zip(units, weights, values):
        out_ref[m, f] = (dot(w, v) * valid_ref[m]).astype(jnp.bfloat16)
    for (n, _, f), w, g in zip(units, weights, masked):
        grad_values = dot(w, g, TN).astype(jnp.bfloat16)
        gva_ref[n, f] = grad_values[:half]
        gvb_ref[n, f] = grad_values[half:]
    for (n, m, f), g in zip(units, grad_scores):
        grad_keys = (dot(g, q_ref[m, f], TN) * inv_root).astype(jnp.bfloat16)
        gka_ref[n, f] = grad_keys[:half]
        gkb_ref[n, f] = grad_keys[half:]


def attend_all(incoming, keys_a, values_a, key_weight, value_weight, query, cot, valid, recv_slot):
    slot_total, rows, width = incoming.shape
    slots = recv_slot.shape[0]
    tokens, features = query.shape
    spans = valid.shape[0]
    column = valid.reshape(tokens, 1)
    weight = pl.BlockSpec((width, CHUNK), lambda j, s: (0, j))
    near = pl.BlockSpec((slots * rows, CHUNK), lambda j, s: (0, j))
    mine = pl.BlockSpec((tokens, CHUNK), lambda j, s: (0, j))
    shape = jax.ShapeDtypeStruct((slots * rows, features), jnp.bfloat16)
    positions = PARTS * slots * rows // spans
    return pl.pallas_call(
        functools.partial(attend_kernel, slots, spans),
        grid_spec=pltpu.PrefetchScalarGridSpec(
            num_scalar_prefetch=1,
            grid=(features // CHUNK,),
            in_specs=[
                pl.BlockSpec((slot_total, rows, width), lambda j, s: (0, 0, 0)),
                near,
                near,
                weight,
                weight,
                mine,
                mine,
                pl.BlockSpec((tokens, 1), lambda j, s: (0, 0)),
            ],
            out_specs=[mine, near, near, near, near],
            scratch_shapes=[pltpu.VMEM((slots * rows, width), jnp.bfloat16)],
        ),
        out_shape=[jax.ShapeDtypeStruct((tokens, features), jnp.bfloat16)] + [shape] * 4,
        cost_estimate=pl.CostEstimate(
            flops=4 * slots * rows * width * features + 10 * tokens * positions * features,
            bytes_accessed=4 * width * features + 12 * slots * rows * features,
            transcendentals=tokens * positions * features // HEAD_DIM,
        ),
        name="attend_all",
    )(recv_slot, incoming, keys_a, values_a, key_weight, value_weight, query, cot, column)


def return_kernel(slots, slot_ref, gk_ref, gv_ref, kw_ref, vw_ref, out_ref, acc):
    step = pl.program_id(0)

    @pl.when(step == 0)
    def _():
        acc[...] = jnp.zeros_like(acc)

    acc[...] += dot(gk_ref[...], kw_ref[...]) + dot(gv_ref[...], vw_ref[...])

    @pl.when(step == pl.num_programs(0) - 1)
    def _():
        rows = out_ref.shape[1]
        for n in range(slots):
            out_ref[slot_ref[n]] = acc[n * rows : (n + 1) * rows].astype(jnp.bfloat16)


def return_part(grad_keys, grad_values, key_weight, value_weight, recv_slot, slot_total):
    slots = recv_slot.shape[0]
    total_rows, features = grad_keys.shape
    rows = total_rows // slots
    width = key_weight.shape[1]
    wide = features // 2
    weight = pl.BlockSpec((wide, width), lambda j, s: (j, 0))
    near = pl.BlockSpec((total_rows, wide), lambda j, s: (0, j))
    return pl.pallas_call(
        functools.partial(return_kernel, slots),
        grid_spec=pltpu.PrefetchScalarGridSpec(
            num_scalar_prefetch=1,
            grid=(features // wide,),
            in_specs=[near, near, weight, weight],
            out_specs=pl.BlockSpec((slot_total, rows, width), lambda j, s: (0, 0, 0)),
            scratch_shapes=[pltpu.VMEM((total_rows, width), jnp.float32)],
        ),
        out_shape=jax.ShapeDtypeStruct((slot_total, rows, width), jnp.bfloat16),
        cost_estimate=pl.CostEstimate(
            flops=4 * total_rows * width * features,
            bytes_accessed=4 * width * features + 4 * total_rows * features,
            transcendentals=0,
        ),
        name="return_part",
    )(recv_slot, grad_keys, grad_values, key_weight, value_weight)


def place_kernel(slot_ref, x_ref, *refs):
    out_ref = refs[-1]
    for n in range(out_ref.shape[0]):
        out_ref[n] = x_ref[slot_ref[n]]


def place(part, returned, send_slot, partial):
    slot_total, rows, width = returned.shape
    count = send_slot.shape[0]
    whole = [] if partial is None else [partial]
    return pl.pallas_call(
        place_kernel,
        grid_spec=pltpu.PrefetchScalarGridSpec(
            num_scalar_prefetch=1,
            grid=(1,),
            in_specs=[pl.BlockSpec((slot_total, rows, width), lambda n, s: (0, 0, 0))]
            + [pl.BlockSpec(memory_space=pl.ANY)] * len(whole),
            out_specs=pl.BlockSpec((count, rows, width), lambda n, s: (0, part, 0)),
        ),
        out_shape=jax.ShapeDtypeStruct((count, PARTS * rows, width), jnp.bfloat16),
        input_output_aliases={2: 0} if whole else {},
        name="place",
    )(send_slot, returned, *whole)


def exchange(block):
    return lax.all_to_all(block, "nbr", split_axis=0, concat_axis=0, tiled=True)


def shards(
    queries,
    cotangent,
    neighbour_tokens,
    neighbour_ids,
    neighbour_dest,
    sequence_ids,
    enc_in,
    enc_out,
    key_weight,
    value_weight,
):
    span_count = sequence_ids.shape[0]
    token_rows, features = queries.shape
    span_len = token_rows // span_count
    head_rows = span_len - 1
    nb_local = neighbour_tokens.shape[0]
    peer_count = lax.axis_size("nbr")
    slot_total = peer_count * CAP

    dest_peer = neighbour_dest // nb_local % peer_count
    earlier = jnp.arange(nb_local)
    same_dest = (dest_peer[:, None] == dest_peer[None, :]) & (earlier[None, :] < earlier[:, None])
    send_slot = dest_peer * CAP + jnp.sum(same_dest.astype(jnp.int32), axis=1)
    slot_ids = neighbour_ids.reshape(-1) % (peer_count * nb_local)
    owners = slot_ids // nb_local
    same_owner = (owners[:, None] == owners[None, :]) & (slot_ids[None, :] < slot_ids[:, None])
    recv_slot = owners * CAP + jnp.sum(same_owner.astype(jnp.int32), axis=1)

    label_send = (sequence_ids[:1] % 128 + 1).astype(jnp.bfloat16)
    label_rows = jnp.broadcast_to(label_send[:, None], (2, features))
    next_rows = from_behind(
        jnp.concatenate([queries[:head_rows], cotangent[:head_rows], label_rows], 0),
        ("seq", "nbr"),
        -1,
    )
    sent_a = encode_part(0, neighbour_tokens, enc_in, enc_out, send_slot, slot_total)
    sent_a, next_rows = lax.optimization_barrier((sent_a, next_rows))
    next_query, next_cot = next_rows[:head_rows], next_rows[head_rows : 2 * head_rows]
    next_label = next_rows[2 * head_rows, :1]
    in_a = exchange(sent_a)
    sent_b = encode_part(1, neighbour_tokens, enc_in, enc_out, send_slot, slot_total)
    in_b = exchange(sent_b)
    own_label = (sequence_ids % 128 + 1).astype(jnp.bfloat16)
    later_label = jnp.concatenate([own_label[1:], next_label], 0)
    offsets = jnp.arange(span_len)
    validity = ((offsets[None, :] == 0) | (own_label[:, None] == later_label[:, None])).astype(
        jnp.float32
    )
    query_ext = jnp.concatenate([queries[head_rows:], next_query], 0)
    cot_ext = jnp.concatenate([cotangent[head_rows:], next_cot], 0)

    keys_a, values_a, key_turned, value_turned = project_part(in_a, key_weight, value_weight, recv_slot)
    extended, gka, gva, gkb, gvb = attend_all(
        in_b, keys_a, values_a, key_weight, value_weight, query_ext, cot_ext, validity, recv_slot
    )
    carried = from_behind(extended[token_rows - head_rows :], ("seq", "nbr"), 1)
    grads_a = return_part(gka, gva, key_turned, value_turned, recv_slot, slot_total)
    grads_a, carried = lax.optimization_barrier((grads_a, carried))
    back_a = exchange(grads_a)
    grads_b = return_part(gkb, gvb, key_turned, value_turned, recv_slot, slot_total)
    back_a, grads_b = lax.optimization_barrier((back_a, grads_b))
    back_b = exchange(grads_b)
    attended = jnp.concatenate([carried, extended[: token_rows - head_rows]], 0)
    grad_encoded = place(1, back_b, send_slot, place(0, back_a, send_slot, None))
    return (attended, grad_encoded)


def solution(mesh):
    in_specs = (
        P(("seq", "nbr"), None),
        P(("seq", "nbr"), None),
        P(("seq", "nbr"), None, None),
        P(("seq", "nbr"), None),
        P(("seq", "nbr")),
        P(("seq", "nbr")),
        P(),
        P(),
        P(),
        P(),
    )
    out_specs = (P(("seq", "nbr"), None), P(("seq", "nbr"), None, None))
    return jax.shard_map(shards, mesh=mesh, in_specs=in_specs, out_specs=out_specs, check_vma=False)
```

```python
import functools
import math

import jax
import jax.numpy as jnp
from jax import lax
from jax.experimental import pallas as pl
from jax.experimental.pallas import tpu as pltpu
from jax.sharding import PartitionSpec as P

HEAD_DIM = 128
CAP = 2
CHUNK = 256
PARTS = 2


epsilon = 1e-06

NT = (((1,), (1,)), ((), ()))
TN = (((0,), (0,)), ((), ()))


def from_behind(block, axis, distance):
    devices = range(lax.axis_size(axis))
    route = [(i - distance, i) for i in devices if i - distance in devices]
    return lax.ppermute(block, axis, route)


def dot(a, b, dims=(((1,), (0,)), ((), ()))):
    return lax.dot_general(a, b, dims, preferred_element_type=jnp.float32)


def encode_kernel(slot_ref, x_ref, in_ref, out_w_ref, out_ref, normed, acc):
    step = pl.program_id(0)
    count, rows, width = x_ref.shape

    @pl.when(step == 0)
    def _():
        inputs = x_ref[...].reshape(count * rows, width).astype(jnp.float32)
        scaling = lax.rsqrt(jnp.mean(inputs * inputs, axis=-1, keepdims=True) + epsilon)
        normed[...] = (inputs * scaling).astype(jnp.bfloat16)
        acc[...] = inputs

    hidden = jax.nn.gelu(dot(normed[...], in_ref[...]), approximate=True).astype(jnp.bfloat16)
    acc[...] += dot(hidden, out_w_ref[...])

    @pl.when(step == pl.num_programs(0) - 1)
    def _():
        for n in range(count):
            out_ref[slot_ref[n]] = acc[n * rows : (n + 1) * rows].astype(jnp.bfloat16)


def encode_part(part, tokens, enc_in, enc_out, send_slot, slot_total):
    count, length, width = tokens.shape
    rows = length // PARTS
    hidden = enc_in.shape[1]
    wide = hidden // 2
    return pl.pallas_call(
        encode_kernel,
        grid_spec=pltpu.PrefetchScalarGridSpec(
            num_scalar_prefetch=1,
            grid=(hidden // wide,),
            in_specs=[
                pl.BlockSpec((count, rows, width), lambda j, s: (0, part, 0)),
                pl.BlockSpec((width, wide), lambda j, s: (0, j)),
                pl.BlockSpec((wide, width), lambda j, s: (j, 0)),
            ],
            out_specs=pl.BlockSpec((slot_total, rows, width), lambda j, s: (0, 0, 0)),
            scratch_shapes=[
                pltpu.VMEM((count * rows, width), jnp.bfloat16),
                pltpu.VMEM((count * rows, width), jnp.float32),
            ],
        ),
        out_shape=jax.ShapeDtypeStruct((slot_total, rows, width), jnp.bfloat16),
        cost_estimate=pl.CostEstimate(
            flops=4 * count * rows * width * hidden,
            bytes_accessed=4 * width * hidden + 6 * count * rows * width,
            transcendentals=count * rows * hidden,
        ),
        name="encode_part",
    )(send_slot, tokens, enc_in, enc_out)


def gather_rows(slot_ref, x_ref, held, slots):
    rows = x_ref.shape[1]
    for n in range(slots):
        held[n * rows : (n + 1) * rows] = x_ref[slot_ref[n]]


def project_kernel(slots, slot_ref, x_ref, kw_ref, vw_ref, k_ref, v_ref, kt_ref, vt_ref, held):
    @pl.when(pl.program_id(0) == 0)
    def _():
        gather_rows(slot_ref, x_ref, held, slots)

    k_ref[...] = dot(held[...], kw_ref[...]).astype(jnp.bfloat16)
    v_ref[...] = dot(held[...], vw_ref[...]).astype(jnp.bfloat16)
    kt_ref[...] = kw_ref[...].T
    vt_ref[...] = vw_ref[...].T


def project_part(incoming, key_weight, value_weight, recv_slot):
    slot_total, rows, width = incoming.shape
    slots = recv_slot.shape[0]
    features = key_weight.shape[1]
    wide = 2 * CHUNK
    weight = pl.BlockSpec((width, wide), lambda j, s: (0, j))
    result = pl.BlockSpec((slots * rows, wide), lambda j, s: (0, j))
    shape = jax.ShapeDtypeStruct((slots * rows, features), jnp.bfloat16)
    turned = pl.BlockSpec((wide, width), lambda j, s: (j, 0))
    turned_shape = jax.ShapeDtypeStruct((features, width), jnp.bfloat16)
    return pl.pallas_call(
        functools.partial(project_kernel, slots),
        grid_spec=pltpu.PrefetchScalarGridSpec(
            num_scalar_prefetch=1,
            grid=(features // wide,),
            in_specs=[
                pl.BlockSpec((slot_total, rows, width), lambda j, s: (0, 0, 0)),
                weight,
                weight,
            ],
            out_specs=[result, result, turned, turned],
            scratch_shapes=[pltpu.VMEM((slots * rows, width), jnp.bfloat16)],
        ),
        out_shape=[shape, shape, turned_shape, turned_shape],
        cost_estimate=pl.CostEstimate(
            flops=4 * slots * rows * width * features,
            bytes_accessed=4 * width * features + 4 * slots * rows * features,
            transcendentals=0,
        ),
        name="project_part",
    )(recv_slot, incoming, key_weight, value_weight)


def attend_kernel(
    slots, spans, slot_ref, x_ref, ka_ref, va_ref, kw_ref, vw_ref, q_ref, c_ref, valid_ref,
    out_ref, sent_ref, gkb_ref, gvb_ref, held, acc, gka_ref, gva_ref,
):
    @pl.when(pl.program_id(0) == 0)
    def _():
        gather_rows(slot_ref, x_ref, held, slots)
        acc[...] = jnp.zeros_like(acc)

    inv_root = 1.0 / math.sqrt(HEAD_DIM)
    kb = dot(held[...], kw_ref[...]).astype(jnp.bfloat16)
    vb = dot(held[...], vw_ref[...]).astype(jnp.bfloat16)
    half = held.shape[0] // spans
    tokens = q_ref.shape[0] // spans
    units = [
        (
            slice(c * half, (c + 1) * half),
            slice(c * tokens, (c + 1) * tokens),
            slice(h * HEAD_DIM, (h + 1) * HEAD_DIM),
        )
        for c in range(spans)
        for h in range(q_ref.shape[1] // HEAD_DIM)
    ]
    keys = [jnp.concatenate([ka_ref[n, f], kb[n, f]], 0) for n, _, f in units]
    values = [jnp.concatenate([va_ref[n, f], vb[n, f]], 0) for n, _, f in units]
    masked = [
        (c_ref[m, f].astype(jnp.float32) * valid_ref[m]).astype(jnp.bfloat16) for _, m, f in units
    ]
    scores = [dot(q_ref[m, f], k, NT) * inv_root for (_, m, f), k in zip(units, keys)]
    grad_weights = [dot(g, v, NT) for g, v in zip(masked, values)]
    powers = [jnp.exp(x - jnp.max(x, axis=-1, keepdims=True)) for x in scores]
    shares = [x * (1.0 / jnp.sum(x, axis=-1, keepdims=True)) for x in powers]
    weights = [x.astype(jnp.bfloat16) for x in shares]
    grad_scores = [
        (x * (g - jnp.sum(x * g, axis=-1, keepdims=True))).astype(jnp.bfloat16)
        for x, g in zip(shares, grad_weights)
    ]
    for (_, m, f), w, v in zip(units, weights, values):
        out_ref[m, f] = (dot(w, v) * valid_ref[m]).astype(jnp.bfloat16)
    for (n, _, f), w, g in zip(units, weights, masked):
        grad_values = dot(w, g, TN).astype(jnp.bfloat16)
        gva_ref[n, f] = grad_values[:half]
        gvb_ref[n, f] = grad_values[half:]
    for (n, m, f), g in zip(units, grad_scores):
        grad_keys = (dot(g, q_ref[m, f], TN) * inv_root).astype(jnp.bfloat16)
        gka_ref[n, f] = grad_keys[:half]
        gkb_ref[n, f] = grad_keys[half:]
    acc[...] += dot(gka_ref[...], kw_ref[...], NT) + dot(gva_ref[...], vw_ref[...], NT)

    @pl.when(pl.program_id(0) == pl.num_programs(0) - 1)
    def _():
        rows = sent_ref.shape[1]
        for n in range(slots):
            sent_ref[slot_ref[n]] = acc[n * rows : (n + 1) * rows].astype(jnp.bfloat16)


def attend_all(incoming, keys_a, values_a, key_weight, value_weight, query, cot, valid, recv_slot):
    slot_total, rows, width = incoming.shape
    slots = recv_slot.shape[0]
    tokens, features = query.shape
    spans = valid.shape[0]
    column = valid.reshape(tokens, 1)
    weight = pl.BlockSpec((width, CHUNK), lambda j, s: (0, j))
    near = pl.BlockSpec((slots * rows, CHUNK), lambda j, s: (0, j))
    mine = pl.BlockSpec((tokens, CHUNK), lambda j, s: (0, j))
    shape = jax.ShapeDtypeStruct((slots * rows, features), jnp.bfloat16)
    positions = PARTS * slots * rows // spans
    return pl.pallas_call(
        functools.partial(attend_kernel, slots, spans),
        grid_spec=pltpu.PrefetchScalarGridSpec(
            num_scalar_prefetch=1,
            grid=(features // CHUNK,),
            in_specs=[
                pl.BlockSpec((slot_total, rows, width), lambda j, s: (0, 0, 0)),
                near,
                near,
                weight,
                weight,
                mine,
                mine,
                pl.BlockSpec((tokens, 1), lambda j, s: (0, 0)),
            ],
            out_specs=[
                mine,
                pl.BlockSpec((slot_total, rows, width), lambda j, s: (0, 0, 0)),
                near,
                near,
            ],
            scratch_shapes=[
                pltpu.VMEM((slots * rows, width), jnp.bfloat16),
                pltpu.VMEM((slots * rows, width), jnp.float32),
                pltpu.VMEM((slots * rows, CHUNK), jnp.bfloat16),
                pltpu.VMEM((slots * rows, CHUNK), jnp.bfloat16),
            ],
        ),
        out_shape=[
            jax.ShapeDtypeStruct((tokens, features), jnp.bfloat16),
            jax.ShapeDtypeStruct((slot_total, rows, width), jnp.bfloat16),
            shape,
            shape,
        ],
        cost_estimate=pl.CostEstimate(
            flops=8 * slots * rows * width * features + 10 * tokens * positions * features,
            bytes_accessed=4 * width * features + 12 * slots * rows * features,
            transcendentals=tokens * positions * features // HEAD_DIM,
        ),
        name="attend_all",
    )(recv_slot, incoming, keys_a, values_a, key_weight, value_weight, query, cot, column)


def return_kernel(slots, slot_ref, gk_ref, gv_ref, kw_ref, vw_ref, out_ref, acc):
    step = pl.program_id(0)

    @pl.when(step == 0)
    def _():
        acc[...] = jnp.zeros_like(acc)

    acc[...] += dot(gk_ref[...], kw_ref[...]) + dot(gv_ref[...], vw_ref[...])

    @pl.when(step == pl.num_programs(0) - 1)
    def _():
        rows = out_ref.shape[1]
        for n in range(slots):
            out_ref[slot_ref[n]] = acc[n * rows : (n + 1) * rows].astype(jnp.bfloat16)


def return_part(grad_keys, grad_values, key_weight, value_weight, recv_slot, slot_total):
    slots = recv_slot.shape[0]
    total_rows, features = grad_keys.shape
    rows = total_rows // slots
    width = key_weight.shape[1]
    wide = features // 2
    weight = pl.BlockSpec((wide, width), lambda j, s: (j, 0))
    near = pl.BlockSpec((total_rows, wide), lambda j, s: (0, j))
    return pl.pallas_call(
        functools.partial(return_kernel, slots),
        grid_spec=pltpu.PrefetchScalarGridSpec(
            num_scalar_prefetch=1,
            grid=(features // wide,),
            in_specs=[near, near, weight, weight],
            out_specs=pl.BlockSpec((slot_total, rows, width), lambda j, s: (0, 0, 0)),
            scratch_shapes=[pltpu.VMEM((total_rows, width), jnp.float32)],
        ),
        out_shape=jax.ShapeDtypeStruct((slot_total, rows, width), jnp.bfloat16),
        cost_estimate=pl.CostEstimate(
            flops=4 * total_rows * width * features,
            bytes_accessed=4 * width * features + 4 * total_rows * features,
            transcendentals=0,
        ),
        name="return_part",
    )(recv_slot, grad_keys, grad_values, key_weight, value_weight)


def place_kernel(slot_ref, x_ref, *refs):
    out_ref = refs[-1]
    for n in range(out_ref.shape[0]):
        out_ref[n] = x_ref[slot_ref[n]]


def place(part, returned, send_slot, partial):
    slot_total, rows, width = returned.shape
    count = send_slot.shape[0]
    whole = [] if partial is None else [partial]
    return pl.pallas_call(
        place_kernel,
        grid_spec=pltpu.PrefetchScalarGridSpec(
            num_scalar_prefetch=1,
            grid=(1,),
            in_specs=[pl.BlockSpec((slot_total, rows, width), lambda n, s: (0, 0, 0))]
            + [pl.BlockSpec(memory_space=pl.ANY)] * len(whole),
            out_specs=pl.BlockSpec((count, rows, width), lambda n, s: (0, part, 0)),
        ),
        out_shape=jax.ShapeDtypeStruct((count, PARTS * rows, width), jnp.bfloat16),
        input_output_aliases={2: 0} if whole else {},
        name="place",
    )(send_slot, returned, *whole)


def exchange(block):
    return lax.all_to_all(block, "nbr", split_axis=0, concat_axis=0, tiled=True)


def shards(
    queries,
    cotangent,
    neighbour_tokens,
    neighbour_ids,
    neighbour_dest,
    sequence_ids,
    enc_in,
    enc_out,
    key_weight,
    value_weight,
):
    span_count = sequence_ids.shape[0]
    token_rows, features = queries.shape
    span_len = token_rows // span_count
    head_rows = span_len - 1
    nb_local = neighbour_tokens.shape[0]
    peer_count = lax.axis_size("nbr")
    slot_total = peer_count * CAP

    dest_peer = neighbour_dest // nb_local % peer_count
    earlier = jnp.arange(nb_local)
    same_dest = (dest_peer[:, None] == dest_peer[None, :]) & (earlier[None, :] < earlier[:, None])
    send_slot = dest_peer * CAP + jnp.sum(same_dest.astype(jnp.int32), axis=1)
    slot_ids = neighbour_ids.reshape(-1) % (peer_count * nb_local)
    owners = slot_ids // nb_local
    same_owner = (owners[:, None] == owners[None, :]) & (slot_ids[None, :] < slot_ids[:, None])
    recv_slot = owners * CAP + jnp.sum(same_owner.astype(jnp.int32), axis=1)

    label_send = (sequence_ids[:1] % 128 + 1).astype(jnp.bfloat16)
    label_rows = jnp.broadcast_to(label_send[:, None], (2, features))
    next_rows = from_behind(
        jnp.concatenate([queries[:head_rows], cotangent[:head_rows], label_rows], 0),
        ("seq", "nbr"),
        -1,
    )
    sent_a = encode_part(0, neighbour_tokens, enc_in, enc_out, send_slot, slot_total)
    sent_a, next_rows = lax.optimization_barrier((sent_a, next_rows))
    next_query, next_cot = next_rows[:head_rows], next_rows[head_rows : 2 * head_rows]
    next_label = next_rows[2 * head_rows, :1]
    in_a = exchange(sent_a)
    sent_b = encode_part(1, neighbour_tokens, enc_in, enc_out, send_slot, slot_total)
    in_b = exchange(sent_b)
    own_label = (sequence_ids % 128 + 1).astype(jnp.bfloat16)
    later_label = jnp.concatenate([own_label[1:], next_label], 0)
    offsets = jnp.arange(span_len)
    validity = ((offsets[None, :] == 0) | (own_label[:, None] == later_label[:, None])).astype(
        jnp.float32
    )
    query_ext = jnp.concatenate([queries[head_rows:], next_query], 0)
    cot_ext = jnp.concatenate([cotangent[head_rows:], next_cot], 0)

    keys_a, values_a, key_turned, value_turned = project_part(in_a, key_weight, value_weight, recv_slot)
    extended, grads_a, gkb, gvb = attend_all(
        in_b, keys_a, values_a, key_weight, value_weight, query_ext, cot_ext, validity, recv_slot
    )
    back_a = exchange(grads_a)
    grads_b = return_part(gkb, gvb, key_turned, value_turned, recv_slot, slot_total)
    grads_b, extended = lax.optimization_barrier((grads_b, extended))
    carried = from_behind(extended[token_rows - head_rows :], ("seq", "nbr"), 1)
    back_a, grads_b, carried = lax.optimization_barrier((back_a, grads_b, carried))
    back_b = exchange(grads_b)
    attended = jnp.concatenate([carried, extended[: token_rows - head_rows]], 0)
    grad_encoded = place(1, back_b, send_slot, place(0, back_a, send_slot, None))
    return (attended, grad_encoded)


def solution(mesh):
    in_specs = (
        P(("seq", "nbr"), None),
        P(("seq", "nbr"), None),
        P(("seq", "nbr"), None, None),
        P(("seq", "nbr"), None),
        P(("seq", "nbr")),
        P(("seq", "nbr")),
        P(),
        P(),
        P(),
        P(),
    )
    out_specs = (P(("seq", "nbr"), None), P(("seq", "nbr"), None, None))
    return jax.shard_map(shards, mesh=mesh, in_specs=in_specs, out_specs=out_specs, check_vma=False)
```

```python
import functools
import math

import jax
import jax.numpy as jnp
from jax import lax
from jax.experimental import pallas as pl
from jax.experimental.pallas import tpu as pltpu
from jax.sharding import PartitionSpec as P

HEAD_DIM = 128
CAP = 2
CHUNK = 256
PARTS = 2


epsilon = 1e-06

NT = (((1,), (1,)), ((), ()))
TN = (((0,), (0,)), ((), ()))


def from_behind(block, axis, distance):
    devices = range(lax.axis_size(axis))
    route = [(i - distance, i) for i in devices if i - distance in devices]
    return lax.ppermute(block, axis, route)


def dot(a, b, dims=(((1,), (0,)), ((), ()))):
    return lax.dot_general(a, b, dims, preferred_element_type=jnp.float32)


def encode_kernel(slot_ref, x_ref, in_ref, out_w_ref, out_ref, normed, acc):
    step = pl.program_id(0)
    count, rows, width = x_ref.shape

    @pl.when(step == 0)
    def _():
        inputs = x_ref[...].reshape(count * rows, width).astype(jnp.float32)
        scaling = lax.rsqrt(jnp.mean(inputs * inputs, axis=-1, keepdims=True) + epsilon)
        normed[...] = (inputs * scaling).astype(jnp.bfloat16)
        acc[...] = inputs

    hidden = jax.nn.gelu(dot(normed[...], in_ref[...]), approximate=True).astype(jnp.bfloat16)
    acc[...] += dot(hidden, out_w_ref[...])

    @pl.when(step == pl.num_programs(0) - 1)
    def _():
        for n in range(count):
            out_ref[slot_ref[n]] = acc[n * rows : (n + 1) * rows].astype(jnp.bfloat16)


def encode_part(part, tokens, enc_in, enc_out, send_slot, slot_total):
    count, length, width = tokens.shape
    rows = length // PARTS
    hidden = enc_in.shape[1]
    wide = hidden // 2
    return pl.pallas_call(
        encode_kernel,
        grid_spec=pltpu.PrefetchScalarGridSpec(
            num_scalar_prefetch=1,
            grid=(hidden // wide,),
            in_specs=[
                pl.BlockSpec((count, rows, width), lambda j, s: (0, part, 0)),
                pl.BlockSpec((width, wide), lambda j, s: (0, j)),
                pl.BlockSpec((wide, width), lambda j, s: (j, 0)),
            ],
            out_specs=pl.BlockSpec((slot_total, rows, width), lambda j, s: (0, 0, 0)),
            scratch_shapes=[
                pltpu.VMEM((count * rows, width), jnp.bfloat16),
                pltpu.VMEM((count * rows, width), jnp.float32),
            ],
        ),
        out_shape=jax.ShapeDtypeStruct((slot_total, rows, width), jnp.bfloat16),
        cost_estimate=pl.CostEstimate(
            flops=4 * count * rows * width * hidden,
            bytes_accessed=4 * width * hidden + 6 * count * rows * width,
            transcendentals=count * rows * hidden,
        ),
        name="encode_part",
    )(send_slot, tokens, enc_in, enc_out)


def gather_rows(slot_ref, x_ref, held, slots):
    rows = x_ref.shape[1]
    for n in range(slots):
        held[n * rows : (n + 1) * rows] = x_ref[slot_ref[n]]


def project_kernel(slots, slot_ref, x_ref, kw_ref, vw_ref, k_ref, v_ref, held):
    @pl.when(pl.program_id(0) == 0)
    def _():
        gather_rows(slot_ref, x_ref, held, slots)

    k_ref[...] = dot(held[...], kw_ref[...]).astype(jnp.bfloat16)
    v_ref[...] = dot(held[...], vw_ref[...]).astype(jnp.bfloat16)


def project_part(incoming, key_weight, value_weight, recv_slot):
    slot_total, rows, width = incoming.shape
    slots = recv_slot.shape[0]
    features = key_weight.shape[1]
    wide = 2 * CHUNK
    weight = pl.BlockSpec((width, wide), lambda j, s: (0, j))
    result = pl.BlockSpec((slots * rows, wide), lambda j, s: (0, j))
    shape = jax.ShapeDtypeStruct((slots * rows, features), jnp.bfloat16)
    return pl.pallas_call(
        functools.partial(project_kernel, slots),
        grid_spec=pltpu.PrefetchScalarGridSpec(
            num_scalar_prefetch=1,
            grid=(features // wide,),
            in_specs=[
                pl.BlockSpec((slot_total, rows, width), lambda j, s: (0, 0, 0)),
                weight,
                weight,
            ],
            out_specs=[result, result],
            scratch_shapes=[pltpu.VMEM((slots * rows, width), jnp.bfloat16)],
        ),
        out_shape=[shape, shape],
        cost_estimate=pl.CostEstimate(
            flops=4 * slots * rows * width * features,
            bytes_accessed=4 * width * features + 4 * slots * rows * features,
            transcendentals=0,
        ),
        name="project_part",
    )(recv_slot, incoming, key_weight, value_weight)


def attend_kernel(
    slots, spans, slot_ref, x_ref, ka_ref, va_ref, kw_ref, vw_ref, q_ref, c_ref, valid_ref,
    out_ref, sent_ref, held, acc, gk_ref, gv_ref,
):
    @pl.when(pl.program_id(0) == 0)
    def _():
        gather_rows(slot_ref, x_ref, held, slots)
        acc[...] = jnp.zeros_like(acc)

    inv_root = 1.0 / math.sqrt(HEAD_DIM)
    kb = dot(held[...], kw_ref[...]).astype(jnp.bfloat16)
    vb = dot(held[...], vw_ref[...]).astype(jnp.bfloat16)
    half = held.shape[0] // spans
    tokens = q_ref.shape[0] // spans
    units = [
        (
            slice(c * half, (c + 1) * half),
            slice(c * tokens, (c + 1) * tokens),
            slice(h * HEAD_DIM, (h + 1) * HEAD_DIM),
        )
        for c in range(spans)
        for h in range(q_ref.shape[1] // HEAD_DIM)
    ]
    keys = [jnp.concatenate([ka_ref[n, f], kb[n, f]], 0) for n, _, f in units]
    values = [jnp.concatenate([va_ref[n, f], vb[n, f]], 0) for n, _, f in units]
    masked = [
        (c_ref[m, f].astype(jnp.float32) * valid_ref[m]).astype(jnp.bfloat16) for _, m, f in units
    ]
    scores = [dot(q_ref[m, f], k, NT) * inv_root for (_, m, f), k in zip(units, keys)]
    grad_weights = [dot(g, v, NT) for g, v in zip(masked, values)]
    powers = [jnp.exp(x - jnp.max(x, axis=-1, keepdims=True)) for x in scores]
    shares = [x * (1.0 / jnp.sum(x, axis=-1, keepdims=True)) for x in powers]
    weights = [x.astype(jnp.bfloat16) for x in shares]
    grad_scores = [
        (x * (g - jnp.sum(x * g, axis=-1, keepdims=True))).astype(jnp.bfloat16)
        for x, g in zip(shares, grad_weights)
    ]
    for (_, m, f), w, v in zip(units, weights, values):
        out_ref[m, f] = (dot(w, v) * valid_ref[m]).astype(jnp.bfloat16)
    for (n, _, f), w, g in zip(units, weights, masked):
        grad_values = dot(w, g, TN).astype(jnp.bfloat16)
        gv_ref[0, n, f] = grad_values[:half]
        gv_ref[1, n, f] = grad_values[half:]
    for (n, m, f), g in zip(units, grad_scores):
        grad_keys = (dot(g, q_ref[m, f], TN) * inv_root).astype(jnp.bfloat16)
        gk_ref[0, n, f] = grad_keys[:half]
        gk_ref[1, n, f] = grad_keys[half:]
    total, wide = acc.shape[0], gk_ref.shape[2]
    grad_keys = gk_ref[...].reshape(total, wide)
    grad_values = gv_ref[...].reshape(total, wide)
    acc[...] += dot(grad_keys, kw_ref[...], NT) + dot(grad_values, vw_ref[...], NT)

    @pl.when(pl.program_id(0) == pl.num_programs(0) - 1)
    def _():
        rows = sent_ref.shape[1] // PARTS
        for part in range(PARTS):
            for n in range(slots):
                at = (part * slots + n) * rows
                sent_ref[slot_ref[n], part * rows : (part + 1) * rows] = acc[
                    at : at + rows
                ].astype(jnp.bfloat16)


def attend_all(incoming, keys_a, values_a, key_weight, value_weight, query, cot, valid, recv_slot):
    slot_total, rows, width = incoming.shape
    slots = recv_slot.shape[0]
    tokens, features = query.shape
    spans = valid.shape[0]
    column = valid.reshape(tokens, 1)
    weight = pl.BlockSpec((width, CHUNK), lambda j, s: (0, j))
    near = pl.BlockSpec((slots * rows, CHUNK), lambda j, s: (0, j))
    mine = pl.BlockSpec((tokens, CHUNK), lambda j, s: (0, j))
    positions = PARTS * slots * rows // spans
    return pl.pallas_call(
        functools.partial(attend_kernel, slots, spans),
        grid_spec=pltpu.PrefetchScalarGridSpec(
            num_scalar_prefetch=1,
            grid=(features // CHUNK,),
            in_specs=[
                pl.BlockSpec((slot_total, rows, width), lambda j, s: (0, 0, 0)),
                near,
                near,
                weight,
                weight,
                mine,
                mine,
                pl.BlockSpec((tokens, 1), lambda j, s: (0, 0)),
            ],
            out_specs=[
                mine,
                pl.BlockSpec((slot_total, PARTS * rows, width), lambda j, s: (0, 0, 0)),
            ],
            scratch_shapes=[
                pltpu.VMEM((slots * rows, width), jnp.bfloat16),
                pltpu.VMEM((PARTS * slots * rows, width), jnp.float32),
                pltpu.VMEM((PARTS, slots * rows, CHUNK), jnp.bfloat16),
                pltpu.VMEM((PARTS, slots * rows, CHUNK), jnp.bfloat16),
            ],
        ),
        out_shape=[
            jax.ShapeDtypeStruct((tokens, features), jnp.bfloat16),
            jax.ShapeDtypeStruct((slot_total, PARTS * rows, width), jnp.bfloat16),
        ],
        cost_estimate=pl.CostEstimate(
            flops=12 * slots * rows * width * features + 10 * tokens * positions * features,
            bytes_accessed=4 * width * features + 12 * slots * rows * features,
            transcendentals=tokens * positions * features // HEAD_DIM,
        ),
        name="attend_all",
    )(recv_slot, incoming, keys_a, values_a, key_weight, value_weight, query, cot, column)


def place_kernel(slot_ref, x_ref, out_ref):
    for n in range(out_ref.shape[0]):
        out_ref[n] = x_ref[slot_ref[n]]


def place(returned, send_slot):
    slot_total, rows, width = returned.shape
    count = send_slot.shape[0]
    strip = rows // 4
    return pl.pallas_call(
        place_kernel,
        grid_spec=pltpu.PrefetchScalarGridSpec(
            num_scalar_prefetch=1,
            grid=(rows // strip,),
            in_specs=[pl.BlockSpec((slot_total, strip, width), lambda n, s: (0, n, 0))],
            out_specs=pl.BlockSpec((count, strip, width), lambda n, s: (0, n, 0)),
        ),
        out_shape=jax.ShapeDtypeStruct((count, rows, width), jnp.bfloat16),
        name="place",
    )(send_slot, returned)


def exchange(block):
    return lax.all_to_all(block, "nbr", split_axis=0, concat_axis=0, tiled=True)


def shards(
    queries,
    cotangent,
    neighbour_tokens,
    neighbour_ids,
    neighbour_dest,
    sequence_ids,
    enc_in,
    enc_out,
    key_weight,
    value_weight,
):
    span_count = sequence_ids.shape[0]
    token_rows, features = queries.shape
    span_len = token_rows // span_count
    head_rows = span_len - 1
    nb_local = neighbour_tokens.shape[0]
    peer_count = lax.axis_size("nbr")
    slot_total = peer_count * CAP

    dest_peer = neighbour_dest // nb_local % peer_count
    earlier = jnp.arange(nb_local)
    same_dest = (dest_peer[:, None] == dest_peer[None, :]) & (earlier[None, :] < earlier[:, None])
    send_slot = dest_peer * CAP + jnp.sum(same_dest.astype(jnp.int32), axis=1)
    slot_ids = neighbour_ids.reshape(-1) % (peer_count * nb_local)
    owners = slot_ids // nb_local
    same_owner = (owners[:, None] == owners[None, :]) & (slot_ids[None, :] < slot_ids[:, None])
    recv_slot = owners * CAP + jnp.sum(same_owner.astype(jnp.int32), axis=1)

    label_send = (sequence_ids[:1] % 128 + 1).astype(jnp.bfloat16)
    label_rows = jnp.broadcast_to(label_send[:, None], (2, features))
    next_rows = from_behind(
        jnp.concatenate([queries[:head_rows], cotangent[:head_rows], label_rows], 0),
        ("seq", "nbr"),
        -1,
    )
    sent_a = encode_part(0, neighbour_tokens, enc_in, enc_out, send_slot, slot_total)
    sent_a, next_rows = lax.optimization_barrier((sent_a, next_rows))
    next_query, next_cot = next_rows[:head_rows], next_rows[head_rows : 2 * head_rows]
    next_label = next_rows[2 * head_rows, :1]
    in_a = exchange(sent_a)
    sent_b = encode_part(1, neighbour_tokens, enc_in, enc_out, send_slot, slot_total)
    in_b = exchange(sent_b)
    own_label = (sequence_ids % 128 + 1).astype(jnp.bfloat16)
    later_label = jnp.concatenate([own_label[1:], next_label], 0)
    offsets = jnp.arange(span_len)
    validity = ((offsets[None, :] == 0) | (own_label[:, None] == later_label[:, None])).astype(
        jnp.float32
    )
    query_ext = jnp.concatenate([queries[head_rows:], next_query], 0)
    cot_ext = jnp.concatenate([cotangent[head_rows:], next_cot], 0)

    keys_a, values_a = project_part(in_a, key_weight, value_weight, recv_slot)
    extended, slot_grads = attend_all(
        in_b, keys_a, values_a, key_weight, value_weight, query_ext, cot_ext, validity, recv_slot
    )
    returned = exchange(slot_grads)
    carried = from_behind(extended[token_rows - head_rows :], ("seq", "nbr"), 1)
    attended = jnp.concatenate([carried, extended[: token_rows - head_rows]], 0)
    grad_encoded = place(returned, send_slot)
    return (attended, grad_encoded)


def solution(mesh):
    in_specs = (
        P(("seq", "nbr"), None),
        P(("seq", "nbr"), None),
        P(("seq", "nbr"), None, None),
        P(("seq", "nbr"), None),
        P(("seq", "nbr")),
        P(("seq", "nbr")),
        P(),
        P(),
        P(),
        P(),
    )
    out_specs = (P(("seq", "nbr"), None), P(("seq", "nbr"), None, None))
    return jax.shard_map(shards, mesh=mesh, in_specs=in_specs, out_specs=out_specs, check_vma=False)
```

```python
import functools
import math

import jax
import jax.numpy as jnp
from jax import lax
from jax.experimental import pallas as pl
from jax.experimental.pallas import tpu as pltpu
from jax.sharding import PartitionSpec as P

HEAD_DIM = 128
CAP = 2
CHUNK = 512
PARTS = 2


epsilon = 1e-06

NT = (((1,), (1,)), ((), ()))
TN = (((0,), (0,)), ((), ()))


def from_behind(block, axis, distance):
    devices = range(lax.axis_size(axis))
    route = [(i - distance, i) for i in devices if i - distance in devices]
    return lax.ppermute(block, axis, route)


def dot(a, b, dims=(((1,), (0,)), ((), ()))):
    return lax.dot_general(a, b, dims, preferred_element_type=jnp.float32)


def encode_kernel(slot_ref, x_ref, in_ref, out_w_ref, out_ref, normed, acc):
    step = pl.program_id(0)
    count, rows, width = x_ref.shape

    @pl.when(step == 0)
    def _():
        inputs = x_ref[...].reshape(count * rows, width).astype(jnp.float32)
        scaling = lax.rsqrt(jnp.mean(inputs * inputs, axis=-1, keepdims=True) + epsilon)
        normed[...] = (inputs * scaling).astype(jnp.bfloat16)
        acc[...] = inputs

    hidden = jax.nn.gelu(dot(normed[...], in_ref[...]), approximate=True).astype(jnp.bfloat16)
    acc[...] += dot(hidden, out_w_ref[...])

    @pl.when(step == pl.num_programs(0) - 1)
    def _():
        for n in range(count):
            out_ref[slot_ref[n]] = acc[n * rows : (n + 1) * rows].astype(jnp.bfloat16)


def encode_part(part, tokens, enc_in, enc_out, send_slot, slot_total):
    count, length, width = tokens.shape
    rows = length // PARTS
    hidden = enc_in.shape[1]
    wide = hidden // 2
    return pl.pallas_call(
        encode_kernel,
        grid_spec=pltpu.PrefetchScalarGridSpec(
            num_scalar_prefetch=1,
            grid=(hidden // wide,),
            in_specs=[
                pl.BlockSpec((count, rows, width), lambda j, s: (0, part, 0)),
                pl.BlockSpec((width, wide), lambda j, s: (0, j)),
                pl.BlockSpec((wide, width), lambda j, s: (j, 0)),
            ],
            out_specs=pl.BlockSpec((slot_total, rows, width), lambda j, s: (0, 0, 0)),
            scratch_shapes=[
                pltpu.VMEM((count * rows, width), jnp.bfloat16),
                pltpu.VMEM((count * rows, width), jnp.float32),
            ],
        ),
        out_shape=jax.ShapeDtypeStruct((slot_total, rows, width), jnp.bfloat16),
        cost_estimate=pl.CostEstimate(
            flops=4 * count * rows * width * hidden,
            bytes_accessed=4 * width * hidden + 6 * count * rows * width,
            transcendentals=count * rows * hidden,
        ),
        name="encode_part",
    )(send_slot, tokens, enc_in, enc_out)


def gather_rows(slot_ref, x_ref, held, slots):
    rows = x_ref.shape[1]
    for n in range(slots):
        held[n * rows : (n + 1) * rows] = x_ref[slot_ref[n]]


def project_kernel(slots, slot_ref, x_ref, kw_ref, vw_ref, k_ref, v_ref, held):
    @pl.when(pl.program_id(0) == 0)
    def _():
        gather_rows(slot_ref, x_ref, held, slots)

    k_ref[...] = dot(held[...], kw_ref[...]).astype(jnp.bfloat16)
    v_ref[...] = dot(held[...], vw_ref[...]).astype(jnp.bfloat16)


def project_part(incoming, key_weight, value_weight, recv_slot):
    slot_total, rows, width = incoming.shape
    slots = recv_slot.shape[0]
    features = key_weight.shape[1]
    wide = CHUNK
    weight = pl.BlockSpec((width, wide), lambda j, s: (0, j))
    result = pl.BlockSpec((slots * rows, wide), lambda j, s: (0, j))
    shape = jax.ShapeDtypeStruct((slots * rows, features), jnp.bfloat16)
    return pl.pallas_call(
        functools.partial(project_kernel, slots),
        grid_spec=pltpu.PrefetchScalarGridSpec(
            num_scalar_prefetch=1,
            grid=(features // wide,),
            in_specs=[
                pl.BlockSpec((slot_total, rows, width), lambda j, s: (0, 0, 0)),
                weight,
                weight,
            ],
            out_specs=[result, result],
            scratch_shapes=[pltpu.VMEM((slots * rows, width), jnp.bfloat16)],
        ),
        out_shape=[shape, shape],
        cost_estimate=pl.CostEstimate(
            flops=4 * slots * rows * width * features,
            bytes_accessed=4 * width * features + 4 * slots * rows * features,
            transcendentals=0,
        ),
        name="project_part",
    )(recv_slot, incoming, key_weight, value_weight)


def attend_kernel(
    slots, spans, slot_ref, x_ref, ka_ref, va_ref, kw_ref, vw_ref, q_ref, c_ref, valid_ref,
    out_ref, sent_ref, held, acc, gk_ref, gv_ref,
):
    @pl.when(pl.program_id(0) == 0)
    def _():
        gather_rows(slot_ref, x_ref, held, slots)
        acc[...] = jnp.zeros_like(acc)

    inv_root = 1.0 / math.sqrt(HEAD_DIM)
    kb = dot(held[...], kw_ref[...]).astype(jnp.bfloat16)
    vb = dot(held[...], vw_ref[...]).astype(jnp.bfloat16)
    half = held.shape[0] // spans
    tokens = q_ref.shape[0] // spans
    units = [
        (
            slice(c * half, (c + 1) * half),
            slice(c * tokens, (c + 1) * tokens),
            slice(h * HEAD_DIM, (h + 1) * HEAD_DIM),
        )
        for c in range(spans)
        for h in range(q_ref.shape[1] // HEAD_DIM)
    ]
    keys = [jnp.concatenate([ka_ref[n, f], kb[n, f]], 0) for n, _, f in units]
    values = [jnp.concatenate([va_ref[n, f], vb[n, f]], 0) for n, _, f in units]
    masked = [
        (c_ref[m, f].astype(jnp.float32) * valid_ref[m]).astype(jnp.bfloat16) for _, m, f in units
    ]
    scores = [dot(q_ref[m, f], k, NT) * inv_root for (_, m, f), k in zip(units, keys)]
    grad_weights = [dot(g, v, NT) for g, v in zip(masked, values)]
    powers = [jnp.exp(x - jnp.max(x, axis=-1, keepdims=True)) for x in scores]
    shares = [x * (1.0 / jnp.sum(x, axis=-1, keepdims=True)) for x in powers]
    weights = [x.astype(jnp.bfloat16) for x in shares]
    grad_scores = [
        (x * (g - jnp.sum(x * g, axis=-1, keepdims=True))).astype(jnp.bfloat16)
        for x, g in zip(shares, grad_weights)
    ]
    for (_, m, f), w, v in zip(units, weights, values):
        out_ref[m, f] = (dot(w, v) * valid_ref[m]).astype(jnp.bfloat16)
    for (n, _, f), w, g in zip(units, weights, masked):
        grad_values = dot(w, g, TN).astype(jnp.bfloat16)
        gv_ref[0, n, f] = grad_values[:half]
        gv_ref[1, n, f] = grad_values[half:]
    for (n, m, f), g in zip(units, grad_scores):
        grad_keys = (dot(g, q_ref[m, f], TN) * inv_root).astype(jnp.bfloat16)
        gk_ref[0, n, f] = grad_keys[:half]
        gk_ref[1, n, f] = grad_keys[half:]
    total, wide = acc.shape[0], gk_ref.shape[2]
    grad_keys = gk_ref[...].reshape(total, wide)
    grad_values = gv_ref[...].reshape(total, wide)
    acc[...] += dot(grad_keys, kw_ref[...], NT) + dot(grad_values, vw_ref[...], NT)

    @pl.when(pl.program_id(0) == pl.num_programs(0) - 1)
    def _():
        rows = sent_ref.shape[1] // PARTS
        for part in range(PARTS):
            for n in range(slots):
                at = (part * slots + n) * rows
                sent_ref[slot_ref[n], part * rows : (part + 1) * rows] = acc[
                    at : at + rows
                ].astype(jnp.bfloat16)


def attend_all(incoming, keys_a, values_a, key_weight, value_weight, query, cot, valid, recv_slot):
    slot_total, rows, width = incoming.shape
    slots = recv_slot.shape[0]
    tokens, features = query.shape
    spans = valid.shape[0]
    column = valid.reshape(tokens, 1)
    weight = pl.BlockSpec((width, CHUNK), lambda j, s: (0, j))
    near = pl.BlockSpec((slots * rows, CHUNK), lambda j, s: (0, j))
    mine = pl.BlockSpec((tokens, CHUNK), lambda j, s: (0, j))
    positions = PARTS * slots * rows // spans
    return pl.pallas_call(
        functools.partial(attend_kernel, slots, spans),
        grid_spec=pltpu.PrefetchScalarGridSpec(
            num_scalar_prefetch=1,
            grid=(features // CHUNK,),
            in_specs=[
                pl.BlockSpec((slot_total, rows, width), lambda j, s: (0, 0, 0)),
                near,
                near,
                weight,
                weight,
                mine,
                mine,
                pl.BlockSpec((tokens, 1), lambda j, s: (0, 0)),
            ],
            out_specs=[
                mine,
                pl.BlockSpec((slot_total, PARTS * rows, width), lambda j, s: (0, 0, 0)),
            ],
            scratch_shapes=[
                pltpu.VMEM((slots * rows, width), jnp.bfloat16),
                pltpu.VMEM((PARTS * slots * rows, width), jnp.float32),
                pltpu.VMEM((PARTS, slots * rows, CHUNK), jnp.bfloat16),
                pltpu.VMEM((PARTS, slots * rows, CHUNK), jnp.bfloat16),
            ],
        ),
        out_shape=[
            jax.ShapeDtypeStruct((tokens, features), jnp.bfloat16),
            jax.ShapeDtypeStruct((slot_total, PARTS * rows, width), jnp.bfloat16),
        ],
        cost_estimate=pl.CostEstimate(
            flops=12 * slots * rows * width * features + 10 * tokens * positions * features,
            bytes_accessed=4 * width * features + 12 * slots * rows * features,
            transcendentals=tokens * positions * features // HEAD_DIM,
        ),
        name="attend_all",
    )(recv_slot, incoming, keys_a, values_a, key_weight, value_weight, query, cot, column)


def place_kernel(slot_ref, x_ref, out_ref):
    for n in range(out_ref.shape[0]):
        out_ref[n] = x_ref[slot_ref[n]]


def place(returned, send_slot):
    slot_total, rows, width = returned.shape
    count = send_slot.shape[0]
    strip = rows // 4
    return pl.pallas_call(
        place_kernel,
        grid_spec=pltpu.PrefetchScalarGridSpec(
            num_scalar_prefetch=1,
            grid=(rows // strip,),
            in_specs=[pl.BlockSpec((slot_total, strip, width), lambda n, s: (0, n, 0))],
            out_specs=pl.BlockSpec((count, strip, width), lambda n, s: (0, n, 0)),
        ),
        out_shape=jax.ShapeDtypeStruct((count, rows, width), jnp.bfloat16),
        name="place",
    )(send_slot, returned)


def exchange(block):
    return lax.all_to_all(block, "nbr", split_axis=0, concat_axis=0, tiled=True)


def shards(
    queries,
    cotangent,
    neighbour_tokens,
    neighbour_ids,
    neighbour_dest,
    sequence_ids,
    enc_in,
    enc_out,
    key_weight,
    value_weight,
):
    span_count = sequence_ids.shape[0]
    token_rows, features = queries.shape
    span_len = token_rows // span_count
    head_rows = span_len - 1
    nb_local = neighbour_tokens.shape[0]
    peer_count = lax.axis_size("nbr")
    slot_total = peer_count * CAP

    dest_peer = neighbour_dest // nb_local % peer_count
    earlier = jnp.arange(nb_local)
    same_dest = (dest_peer[:, None] == dest_peer[None, :]) & (earlier[None, :] < earlier[:, None])
    send_slot = dest_peer * CAP + jnp.sum(same_dest.astype(jnp.int32), axis=1)
    slot_ids = neighbour_ids.reshape(-1) % (peer_count * nb_local)
    owners = slot_ids // nb_local
    same_owner = (owners[:, None] == owners[None, :]) & (slot_ids[None, :] < slot_ids[:, None])
    recv_slot = owners * CAP + jnp.sum(same_owner.astype(jnp.int32), axis=1)

    label_send = (sequence_ids[:1] % 128 + 1).astype(jnp.bfloat16)
    label_rows = jnp.broadcast_to(label_send[:, None], (2, features))
    next_rows = from_behind(
        jnp.concatenate([queries[:head_rows], cotangent[:head_rows], label_rows], 0),
        ("seq", "nbr"),
        -1,
    )
    sent_a = encode_part(0, neighbour_tokens, enc_in, enc_out, send_slot, slot_total)
    sent_a, next_rows = lax.optimization_barrier((sent_a, next_rows))
    next_query, next_cot = next_rows[:head_rows], next_rows[head_rows : 2 * head_rows]
    next_label = next_rows[2 * head_rows, :1]
    in_a = exchange(sent_a)
    sent_b = encode_part(1, neighbour_tokens, enc_in, enc_out, send_slot, slot_total)
    in_b = exchange(sent_b)
    own_label = (sequence_ids % 128 + 1).astype(jnp.bfloat16)
    later_label = jnp.concatenate([own_label[1:], next_label], 0)
    offsets = jnp.arange(span_len)
    validity = ((offsets[None, :] == 0) | (own_label[:, None] == later_label[:, None])).astype(
        jnp.float32
    )
    query_ext = jnp.concatenate([queries[head_rows:], next_query], 0)
    cot_ext = jnp.concatenate([cotangent[head_rows:], next_cot], 0)

    keys_a, values_a = project_part(in_a, key_weight, value_weight, recv_slot)
    extended, slot_grads = attend_all(
        in_b, keys_a, values_a, key_weight, value_weight, query_ext, cot_ext, validity, recv_slot
    )
    returned = exchange(slot_grads)
    carried = from_behind(extended[token_rows - head_rows :], ("seq", "nbr"), 1)
    attended = jnp.concatenate([carried, extended[: token_rows - head_rows]], 0)
    grad_encoded = place(returned, send_slot)
    return (attended, grad_encoded)


def solution(mesh):
    in_specs = (
        P(("seq", "nbr"), None),
        P(("seq", "nbr"), None),
        P(("seq", "nbr"), None, None),
        P(("seq", "nbr"), None),
        P(("seq", "nbr")),
        P(("seq", "nbr")),
        P(),
        P(),
        P(),
        P(),
    )
    out_specs = (P(("seq", "nbr"), None), P(("seq", "nbr"), None, None))
    return jax.shard_map(shards, mesh=mesh, in_specs=in_specs, out_specs=out_specs, check_vma=False)
```
